32 devices in a mesh: row: 4 (over y, core), col: 8 (over z, x).
Axes of the slice: x: 2, y: 2, z: 4, core: 2. Of those that a mesh axis runs over, the one named last changes fastest.
Arguments:
- coeffs: float32 [2048, 2048], P('row', 'col'), may hold values from -8 to 8, as said below
- features: float32 [2048, 512], P('row'), may hold values from -0.6 to 0.6
- factors: float32 [2048, 256], P('row'), may hold values from -1.8 to 1.8
Outputs:
- grad_coeffs: float32 [2048, 2048], P('row', 'col')
- grad_features: float32 [2048, 512], P('row', 'col')
The draws below stay inside these ranges and needn't reach their ends.
Inputs may be any that keep to these rules, and one draw needn't show every extreme that they name: `coeffs`: real coefficients.
All inputs are finite; a program needn't handle non-finite values.
Results may differ from the reference program's by a relative error of at most 0.0003.
Values sent between devices are 32-bit elements; how exact they have to be, the bound alone decides.
No kernel may reach another device: no remote copies, remote signals or barrier semaphores. Data moves between devices by JAX's collectives and lax.ppermute only.
A program may use at most 64 MiB of HBM per device.

```python
import math
import jax
import jax.numpy as jnp
from jax import lax

F = 512
K = 256
SAMPLES = 2048


def draw_coeffs(key, part):
    first, second, third = jax.random.split(jax.random.fold_in(key, 17), 3)
    shape = (SAMPLES, SAMPLES)
    background = jax.random.normal(first, shape, jnp.float32)
    picked = jax.random.bernoulli(second, 8.0 / SAMPLES, shape)
    paired = jnp.logical_or(picked, picked.T)
    heavy = jax.random.uniform(third, shape, jnp.float32, -1.5, 1.5)
    values = background * (3.0 * SAMPLES ** (-0.5)) + jnp.where(paired, heavy, 0.0)
    return values.astype(jnp.float32)


def block_scale(stream_key, dims, cuts, low, high):
    factor_of, own = 1.0, jax.random.fold_in(stream_key, 6)
    for dim, parts in cuts:
        steps = jnp.exp(jax.random.uniform(jax.random.fold_in(own, dim), (parts,), jnp.float32, low / len(cuts), high / len(cuts)))
        factor_of = factor_of * jnp.repeat(steps, dims[dim] // parts).reshape([-1 if axis == dim else 1 for axis in range(len(dims))])
    return factor_of


def normal_values(key, extent, deviation, most, cuts=(), kind=jnp.bfloat16):
    array = deviation * jax.random.normal(key, extent, jnp.float32)
    if cuts:
        array = array * block_scale(key, extent, cuts, -0.22, 0.18)
    return jnp.clip(array, -most, most).astype(kind)


def setup_inputs(seed: int = 0) -> dict:
    arg_keys = jax.random.split(jax.random.key(seed), 4)
    coeffs = draw_coeffs(jax.random.fold_in(arg_keys[3], 71), 0)
    features = normal_values(arg_keys[1], (SAMPLES, F), 0.1, 0.6, ((0, 4),), jnp.float32)
    factors = normal_values(arg_keys[2], (SAMPLES, K), 0.3, 1.8, ((0, 4),), jnp.float32)
    return dict(coeffs=coeffs, features=features, factors=factors)


def reference(coeffs, features, factors):
    highest = lax.Precision.HIGHEST
    residual = jnp.dot(coeffs, features, precision=highest, preferred_element_type=jnp.float32) - features
    grad_features = jnp.dot(coeffs.T, residual, precision=highest, preferred_element_type=jnp.float32) - residual
    block_rows = math.gcd(SAMPLES, 512)

    def one_block(row_start):
        row_start = row_start.astype(jnp.int32)
        rows = lax.dynamic_slice_in_dim(coeffs, row_start, block_rows, 0)
        mirrored = lax.dynamic_slice_in_dim(coeffs, row_start, block_rows, 1).T
        symmetric = 0.5 * (rows * rows + mirrored * mirrored)
        own_factors = lax.dynamic_slice_in_dim(factors, row_start, block_rows, 0)
        relation = symmetric - jnp.dot(own_factors, factors.T, precision=highest, preferred_element_type=jnp.float32)
        own_residual = lax.dynamic_slice_in_dim(residual, row_start, block_rows, 0)
        outer = jnp.dot(own_residual, features.T, precision=highest, preferred_element_type=jnp.float32)
        return outer + 2.0 * rows * relation

    starts = jnp.arange(SAMPLES // block_rows, dtype=jnp.int32) * block_rows
    grad_coeffs = lax.map(one_block, starts).reshape(SAMPLES, SAMPLES)
    return grad_coeffs, grad_features
```

```python
import jax
import jax.numpy as jnp
from jax import lax
from jax.sharding import PartitionSpec as P

AXES = ("row", "col")
HIGH = lax.Precision.HIGH


def dot(left, right, left_dim, right_dim):
    return lax.dot_general(
        left,
        right,
        (((left_dim,), (right_dim,)), ((), ())),
        precision=HIGH,
        preferred_element_type=jnp.float32,
    )


def after(value, *others):
    return lax.optimization_barrier((value, *others))[0]


def rows_of(array, start, count):
    return lax.dynamic_slice_in_dim(array, start, count, 0)


def per_device(coeffs, features, factors):
    row_count = lax.axis_size("row")
    col_count = lax.axis_size("col")
    fold = col_count // row_count
    r = lax.axis_index("row")
    col = lax.axis_index("col")
    q, b = col // fold, col % fold
    own_rows, own_cols = coeffs.shape
    width = features.shape[1]
    quarter = own_rows // row_count
    piece = quarter // fold
    bits = [1 << n for n in range(row_count.bit_length() - 1)]

    def send(value, route):
        pairs = []
        for i in range(row_count):
            for j in range(row_count):
                for k in range(fold):
                    to = route(i, j, k)
                    if to is not None:
                        pairs.append(
                            (i * col_count + j * fold + k, to[0] * col_count + to[1] * fold + to[2])
                        )
        return lax.ppermute(value, AXES, pairs)

    def identity(row_start, col_start, shape):
        rows = row_start + lax.broadcasted_iota(jnp.int32, shape, 0)
        cols = col_start + lax.broadcasted_iota(jnp.int32, shape, 1)
        return (rows == cols).astype(jnp.float32)

    held = rows_of(features, b * own_cols, own_cols)[None]
    gathered = {0: held}
    names = [0]
    for bit in reversed(bits):
        with jax.named_scope(f"feat{bit}"):
            got = send(held, lambda i, j, k, bit=bit: (i ^ bit, j, k))
            held = jnp.concatenate([held, got], 0)
            names = names + [n | bit for n in names]
    block_features = held

    pieces = []
    for s in range(row_count):
        part = rows_of(coeffs, (q ^ s) * quarter, quarter)
        if s:
            with jax.named_scope(f"coef{s}"):
                part = send(part, lambda i, j, k, s=s: (i, j ^ s, k))
        start = ((q ^ s) * fold + b) * own_cols
        pieces.append(part - identity(r * own_rows + q * quarter, start, part.shape))
    stacked = jnp.stack(pieces)
    lhs = jnp.concatenate(
        [lax.dynamic_index_in_dim(stacked, q ^ r ^ t, 0, keepdims=False) for t in names], 1
    )
    rhs = block_features.reshape(row_count * own_cols, width)

    def mirror_part(d, *deps):
        part = rows_of(coeffs, (b ^ d) * own_cols, own_cols)
        part = after(part, *deps)
        with jax.named_scope(f"mirror{d}"):
            return send(part, lambda i, j, k: (j, i, k ^ d))

    mirrored = [mirror_part(0, stacked)]

    col_factors = rows_of(factors, b * own_cols, own_cols)
    for n, bit in enumerate(reversed(bits)):
        if n == 0:
            col_factors = after(col_factors, block_features)
        with jax.named_scope(f"fact{bit}"):
            got = send(
                col_factors,
                lambda i, j, k, bit=bit: (i ^ bit, j, k) if (i ^ j) & (2 * bit - 1) == 0 else None,
            )
        take = ((r ^ q) & (2 * bit - 1)) == bit
        col_factors = jnp.where(take, got, col_factors)

    share = None
    for d in reversed(range(fold)):
        part = dot(rows_of(lhs, (b ^ d) * piece, piece), rhs, 1, 0)
        if d:
            with jax.named_scope(f"resid{d}"):
                part = send(part, lambda i, j, k, d=d: (i, j, k ^ d))
        share = part if share is None else share + part

    chunks = []
    for s in range(row_count):
        one = share
        if s:
            with jax.named_scope(f"gath{s}"):
                one = send(share, lambda i, j, k, s=s: (i, j ^ s, k))
        chunks.append(one)
    spread = []
    for s in range(row_count):
        for d in range(fold):
            one = chunks[s]
            if d:
                with jax.named_scope(f"forw{s}_{d}"):
                    one = send(one, lambda i, j, k, d=d: (i, j, k ^ d))
            spread.append(one)
    residual = jnp.concatenate(spread, 0)
    mirrored += [mirror_part(d, *chunks) for d in range(1, fold)]

    less_one = coeffs - identity(r * own_rows, col * own_cols, coeffs.shape)
    shuffled = jnp.concatenate(
        [
            rows_of(less_one, (q ^ s) * quarter + (b ^ d) * piece, piece)
            for s in range(row_count)
            for d in range(fold)
        ],
        0,
    )
    total = dot(residual, shuffled, 0, 0)
    for bit in bits:
        half = total.shape[0] // 2
        mine = (r & bit) // bit
        with jax.named_scope(f"tail{bit}"):
            got = send(
                rows_of(total, (1 - mine) * half, half), lambda i, j, k, bit=bit: (i ^ bit, j, k)
            )
        total = rows_of(total, mine * half, half) + got

    def turned(i):
        out = 0
        for bit in bits:
            out = 2 * out + (i & bit) // bit
        return out

    share_width = width // col_count
    placed = []
    for d in range(fold):
        with jax.named_scope(f"exch{d}"):
            placed.append(
                send(
                    rows_of(total, (b ^ d) * share_width, share_width),
                    lambda i, j, k, d=d: (j, turned(i), k ^ d),
                )
            )
    placed = jnp.stack(placed)
    grad_features = jnp.concatenate(
        [lax.dynamic_index_in_dim(placed, b ^ e, 0, keepdims=False) for e in range(fold)], 1
    ).T

    own_features = lax.dynamic_index_in_dim(block_features, names.index(0), 0, keepdims=False)
    order = jnp.array(names, jnp.int32)
    stored = jnp.array([names.index(t) for t in range(row_count)], jnp.int32)
    own_features = lax.dynamic_index_in_dim(block_features, stored[r ^ q], 0, keepdims=False)
    outer = dot(residual, own_features, 1, 1)
    outer = jnp.concatenate(
        [
            rows_of(outer, (j ^ q) * quarter + (e ^ b) * piece, piece)
            for j in range(row_count)
            for e in range(fold)
        ],
        0,
    )
    mirrored = jnp.stack(mirrored)
    mirrored = jnp.concatenate(
        [lax.dynamic_index_in_dim(mirrored, b ^ e, 0, keepdims=False).T for e in range(fold)], 0
    )
    symmetric = 0.5 * (coeffs * coeffs + mirrored * mirrored)
    relation = symmetric - dot(factors, col_factors, 1, 1)
    grad_coeffs = outer + 2.0 * coeffs * relation
    return (grad_coeffs, grad_features)


def solution(mesh):
    in_specs = (P("row", "col"), P("row", None), P("row", None))
    out_specs = (P("row", "col"), P("row", "col"))
    return jax.shard_map(
        per_device, mesh=mesh, in_specs=in_specs, out_specs=out_specs, check_vma=False
    )
```

```python
import functools
import jax
import jax.numpy as jnp
from jax import lax
from jax.experimental import pallas as pl
from jax.experimental.pallas import tpu as pltpu
from jax.sharding import PartitionSpec as P

AXES = ("row", "col")
F32, BF16 = jnp.float32, jnp.bfloat16


def after(value, *others):
    return lax.optimization_barrier((value, *others))[0]


def split(value):
    high = value.astype(BF16)
    return high, (value - high.astype(F32)).astype(BF16)


def dot3(left, right, left_dim, right_dim):
    def one(a, b):
        return lax.dot_general(
            a, b, (((left_dim,), (right_dim,)), ((), ())), preferred_element_type=F32
        )

    return one(left[0], right[0]) + (one(left[0], right[1]) + one(left[1], right[0]))


def place(fold):
    col = lax.axis_index("col")
    return lax.axis_index("row"), lax.div(col, fold), lax.rem(col, fold)


def identity(first, shape):
    rows = lax.broadcasted_iota(jnp.int32, shape, 0)
    cols = lax.broadcasted_iota(jnp.int32, shape, 1)
    return jnp.where(rows - cols == first, 1.0, 0.0)


def rows_at(start, count):
    return pl.ds(pl.multiple_of(start, count), count)


def call(kernel, name, outs, args, scratch=(), flops=0, hbm=()):
    moved = sum(4 * a.size for a in args) + sum(4 * o.size for o in outs)
    any_or_vmem = [
        pl.BlockSpec(memory_space=pl.ANY if n in hbm else pltpu.VMEM) for n in range(len(args))
    ]
    return pl.pallas_call(
        kernel,
        name=name,
        out_shape=outs,
        in_specs=any_or_vmem,
        out_specs=[pl.BlockSpec(memory_space=pltpu.VMEM) for _ in outs],
        scratch_shapes=list(scratch),
        cost_estimate=pl.CostEstimate(flops=flops, bytes_accessed=moved, transcendentals=0),
    )(*args)


def shape(*dims, dtype=F32):
    return jax.ShapeDtypeStruct(dims, dtype)


def cut_kernel(cuts, fold, *refs):
    count = max(cut[0] for cut in cuts) + 1
    ins, outs, sems = refs[:count], refs[count:-1], refs[-1]
    r, q, b = place(fold)
    copies = []
    for n, (source, rows, block) in enumerate(cuts):
        copies.append(
            pltpu.make_async_copy(
                ins[source].at[rows_at(block(r, q, b) * rows, rows)], outs[n], sems.at[n]
            )
        )
    for copy in copies:
        copy.start()
    for copy in copies:
        copy.wait()


def cut_rows(name, arrays, cuts, fold):
    outs = [shape(rows, arrays[source].shape[1]) for source, rows, _ in cuts]
    return call(
        functools.partial(cut_kernel, cuts, fold),
        name,
        outs,
        arrays,
        scratch=[pltpu.SemaphoreType.DMA((len(cuts),))],
        hbm=range(len(arrays)),
    )


def residual_kernel(count, fold, *refs):
    parts, blocks, outs, total = refs[:count], refs[count : 2 * count], refs[2 * count : -1], refs[-1]
    r, q, b = place(fold)
    quarter, own_cols = parts[0].shape
    piece = quarter // fold
    for t in range(count):
        wanted = q ^ r ^ t
        left = parts[0][...]
        for s in range(1, count):
            left = jnp.where(wanted == s, parts[s][...], left)
        if t == 0:
            left = left - identity(b * own_cols - q * quarter, left.shape)
        product = dot3(split(left), split(blocks[t][...]), 1, 0)
        if t == 0:
            total[...] = product
        else:
            total[...] += product
    for d in range(fold):
        outs[d][...] = total[rows_at((b ^ d) * piece, piece)]


def project_kernel(count, fold, *refs):
    chunks, coeffs = refs[: count * fold], refs[count * fold]
    give, keep, high, low = refs[count * fold + 1 : count * fold + 5]
    total = refs[-1]
    r, q, b = place(fold)
    piece = chunks[0].shape[0]
    for s in range(count):
        for d in range(fold):
            at = rows_at(((q ^ s) * fold + (b ^ d)) * piece, piece)
            high[at], low[at] = split(chunks[s * fold + d][...])
    own_rows, own_cols = coeffs.shape
    less_one = coeffs[...] - identity((q * fold + b) * own_cols - r * own_rows, coeffs.shape)
    total[...] = dot3((high[...], low[...]), split(less_one), 0, 0)
    half = give.shape[0]
    mine = r & 1
    give[...] = total[rows_at((1 - mine) * half, half)]
    keep[...] = total[rows_at(mine * half, half)]


def halve_kernel(bit, fold, old_ref, got_ref, give, keep, total):
    r, _, _ = place(fold)
    total[...] = old_ref[...] + got_ref[...]
    half = give.shape[0]
    mine = lax.rem(lax.div(r, bit), 2)
    give[...] = total[rows_at((1 - mine) * half, half)]
    keep[...] = total[rows_at(mine * half, half)]


def share_kernel(fold, old_ref, got_ref, *refs):
    outs, total = refs[:-1], refs[-1]
    _, _, b = place(fold)
    total[...] = old_ref[...] + got_ref[...]
    width = outs[0].shape[0]
    for d in range(fold):
        outs[d][...] = total[rows_at((b ^ d) * width, width)]


def finish_kernel(fold, *refs):
    parts, out = refs[:fold], refs[fold]
    _, _, b = place(fold)
    cols = parts[0].shape[1]
    for e in range(fold):
        value = parts[0][...]
        for d in range(1, fold):
            value = jnp.where((b ^ e) == d, parts[d][...], value)
        out[:, e * cols : (e + 1) * cols] = value


def coeff_kernel(count, fold, *refs):
    high, low, coeffs, factors, col_factors = refs[:5]
    blocks, mirrored, out = refs[5 : 5 + count], refs[5 + count : 5 + count + fold], refs[-1]
    r, q, b = place(fold)
    features = blocks[0][...]
    for t in range(1, count):
        features = jnp.where((r ^ q) == t, blocks[t][...], features)
    features = split(features)
    right = split(col_factors[...])
    rows = mirrored[0].shape[0]
    for e in range(fold):
        at = slice(e * rows, (e + 1) * rows)
        turned = mirrored[0][...]
        for d in range(1, fold):
            turned = jnp.where((b ^ e) == d, mirrored[d][...], turned)
        turned = turned.T
        own = coeffs[at]
        symmetric = 0.5 * (own * own + turned * turned)
        relation = symmetric - dot3(split(factors[at]), right, 1, 1)
        outer = dot3((high[at], low[at]), features, 1, 1)
        out[at] = outer + 2.0 * own * relation


def per_device(coeffs, features, factors):
    row_count = lax.axis_size("row")
    col_count = lax.axis_size("col")
    fold = col_count // row_count
    r = lax.axis_index("row")
    q = lax.axis_index("col") // fold
    own_rows, own_cols = coeffs.shape
    width = features.shape[1]
    quarter = own_rows // row_count
    piece = quarter // fold
    bits = [1 << n for n in range(row_count.bit_length() - 1)]
    every, both = range(row_count), range(fold)

    def send(name, value, route):
        pairs = []
        for i in every:
            for j in every:
                for k in both:
                    to = route(i, j, k)
                    if to is not None:
                        start = i * col_count + j * fold + k
                        pairs.append((start, to[0] * col_count + to[1] * fold + to[2]))
        with jax.named_scope(name):
            return lax.ppermute(value, AXES, pairs)

    blocks = {0: cut_rows("cut_features", [features], [(0, own_cols, lambda r, q, b: b)], fold)[0]}
    for bit in reversed(bits):
        for t in list(blocks):
            blocks[t | bit] = send(f"feat{t | bit}", blocks[t], lambda i, j, k: (i ^ bit, j, k))
    blocks = [blocks[t] for t in every]

    cuts = [(0, quarter, lambda r, q, b, s=s: q ^ s) for s in every]
    cuts += [(0, own_cols, lambda r, q, b, d=d: b ^ d) for d in both]
    cuts += [(1, own_cols, lambda r, q, b: b)]
    cut = cut_rows("cut_coeffs", [coeffs, factors], cuts, fold)
    parts, turns, col_factors = cut[:row_count], cut[row_count:-1], cut[-1]
    parts = [
        send(f"coef{s}", parts[s], lambda i, j, k: (i, j ^ s, k)) if s else parts[s] for s in every
    ]

    def mirror(d, *deps):
        return send(f"mirror{d}", after(turns[d], *deps), lambda i, j, k: (j, i, k ^ d))

    mirrored = {fold - 1: mirror(fold - 1, *parts)}

    shares = call(
        functools.partial(residual_kernel, row_count, fold),
        "residual",
        [shape(piece, width)] * fold,
        [*parts, *blocks],
        scratch=[pltpu.VMEM((quarter, width), F32)],
        flops=6 * quarter * row_count * own_cols * width,
    )
    share = shares[0]
    for d in range(1, fold):
        share = share + send(f"resid{d}", shares[d], lambda i, j, k: (i, j, k ^ d))

    col_factors = after(col_factors, *blocks)
    for bit in reversed(bits):
        got = send(
            f"fact{bit}",
            col_factors,
            lambda i, j, k: (i ^ bit, j, k) if (i ^ j) & (2 * bit - 1) == 0 else None,
        )
        col_factors = jnp.where(((r ^ q) & (2 * bit - 1)) == bit, got, col_factors)

    chunks = [
        send(f"gath{s}", share, lambda i, j, k: (i, j ^ s, k)) if s else share for s in every
    ]
    spread = []
    for s in every:
        for d in both:
            one = chunks[s]
            spread.append(send(f"forw{s}_{d}", one, lambda i, j, k: (i, j, k ^ d)) if d else one)
    for d in range(fold - 1):
        mirrored[d] = mirror(d, *chunks)

    give, keep, high, low = call(
        functools.partial(project_kernel, row_count, fold),
        "project",
        [shape(width // 2, own_cols)] * 2 + [shape(own_rows, width, dtype=BF16)] * 2,
        [*spread, coeffs],
        scratch=[pltpu.VMEM((width, own_cols), F32)],
        flops=6 * own_rows * own_cols * width,
    )
    for bit in bits:
        got = send(f"tail{bit}", give, lambda i, j, k: (i ^ bit, j, k))
        rows = got.shape[0]
        total = pltpu.VMEM((rows, own_cols), F32)
        if bit != bits[-1]:
            give, keep = call(
                functools.partial(halve_kernel, 2 * bit, fold),
                "halve",
                [shape(rows // 2, own_cols)] * 2,
                [keep, got],
                scratch=[total],
            )
    pieces = call(
        functools.partial(share_kernel, fold),
        "share",
        [shape(rows // fold, own_cols)] * fold,
        [keep, got],
        scratch=[total],
    )

    def turned(i):
        out = 0
        for bit in bits:
            out = 2 * out + (i // bit) % 2
        return out

    placed = [
        send(f"exch{d}", pieces[d], lambda i, j, k: (j, turned(i), k ^ d)) for d in both
    ]
    grad_features = call(
        functools.partial(finish_kernel, fold),
        "finish",
        [shape(rows // fold, own_rows)],
        placed,
    )[0].T

    grad_coeffs = call(
        functools.partial(coeff_kernel, row_count, fold),
        "coeff",
        [shape(own_rows, own_cols)],
        [high, low, coeffs, factors, col_factors, *blocks, *[mirrored[d] for d in both]],
        flops=6 * own_rows * own_cols * (width + factors.shape[1]),
    )[0]
    return (grad_coeffs, grad_features)


def solution(mesh):
    in_specs = (P("row", "col"), P("row", None), P("row", None))
    out_specs = (P("row", "col"), P("row", "col"))
    return jax.shard_map(
        per_device, mesh=mesh, in_specs=in_specs, out_specs=out_specs, check_vma=False
    )
```

```python
import functools
import jax
import jax.numpy as jnp
from jax import lax
from jax.experimental import pallas as pl
from jax.experimental.pallas import tpu as pltpu
from jax.sharding import PartitionSpec as P


AXES = ("row", "col")
F32, BF16 = jnp.float32, jnp.bfloat16


def after(value, *others):
    return lax.optimization_barrier((value, *others))[0]


def split(value):
    high = value.astype(BF16)
    return high, (value - high.astype(F32)).astype(BF16)


def dot3(left, right, left_dim, right_dim):
    def one(a, b):
        return lax.dot_general(
            a, b, (((left_dim,), (right_dim,)), ((), ())), preferred_element_type=F32
        )

    return one(left[0], right[0]) + (one(left[0], right[1]) + one(left[1], right[0]))


def place(fold):
    col = lax.axis_index("col")
    return lax.axis_index("row"), lax.div(col, fold), lax.rem(col, fold)


def identity(first, shape):
    rows = lax.broadcasted_iota(jnp.int32, shape, 0)
    cols = lax.broadcasted_iota(jnp.int32, shape, 1)
    return jnp.where(rows - cols == first, 1.0, 0.0)


def rows_at(start, count):
    return pl.ds(pl.multiple_of(start, count), count)


def call(kernel, outs, args, scratch=(), flops=0, hbm=(), grant=2):
    moved = sum(4 * a.size for a in args) + sum(4 * o.size for o in outs)
    spaces = [pltpu.HBM if n in hbm else pltpu.VMEM for n in range(len(args))]
    return pl.pallas_call(
        kernel,
        out_shape=outs,
        in_specs=[pl.BlockSpec(memory_space=space) for space in spaces],
        out_specs=[pl.BlockSpec(memory_space=pltpu.VMEM) for _ in outs],
        scratch_shapes=list(scratch),
        compiler_params=pltpu.CompilerParams(vmem_limit_bytes=grant << 20),
        cost_estimate=pl.CostEstimate(flops=flops, bytes_accessed=moved, transcendentals=0),
    )(*args)


def shape(*dims, dtype=F32):
    return jax.ShapeDtypeStruct(dims, dtype)


def cut_kernel(cuts, fold, *refs):
    count = max(cut[0] for cut in cuts) + 1
    ins, outs, sems = refs[:count], refs[count:-1], refs[-1]
    r, q, b = place(fold)
    copies = []
    for n, (source, rows, block) in enumerate(cuts):
        copies.append(
            pltpu.make_async_copy(
                ins[source].at[rows_at(block(r, q, b) * rows, rows)], outs[n], sems.at[n]
            )
        )
    for copy in copies:
        copy.start()
    for copy in copies:
        copy.wait()


def cut_rows(arrays, cuts, fold):
    outs = [shape(rows, arrays[source].shape[1]) for source, rows, _ in cuts]
    return call(
        functools.partial(cut_kernel, cuts, fold),
        outs,
        arrays,
        scratch=[pltpu.SemaphoreType.DMA((len(cuts),))],
        hbm=range(len(arrays)),
    )


def residual_kernel(count, fold, *refs):
    parts, blocks, outs, total = refs[:count], refs[count : 2 * count], refs[2 * count : -1], refs[-1]
    r, q, b = place(fold)
    quarter, own_cols = parts[0].shape
    piece = quarter // fold
    for t in range(count):
        wanted = q ^ r ^ t
        left = parts[0][...]
        for s in range(1, count):
            left = jnp.where(wanted == s, parts[s][...], left)
        if t == 0:
            left = left - identity(b * own_cols - q * quarter, left.shape)
        product = dot3(split(left), split(blocks[t][...]), 1, 0)
        if t == 0:
            total[...] = product
        else:
            total[...] += product
    for d in range(fold):
        outs[d][...] = total[rows_at((b ^ d) * piece, piece)]


def assemble(chunks, high, low, fold, q, b):
    piece = chunks[0].shape[0]
    for n, chunk in enumerate(chunks):
        at = rows_at(((q ^ (n // fold)) * fold + (b ^ (n % fold))) * piece, piece)
        high[at], low[at] = split(chunk[...])


def add_kernel(left, right, out):
    out[...] = left[...] + right[...]


def pick_kernel(bit, fold, old_ref, got_ref, out):
    r, q, _ = place(fold)
    out[...] = jnp.where(((r ^ q) & (2 * bit - 1)) == bit, got_ref[...], old_ref[...])


def project_kernel(count, fold, *refs):
    chunks, coeffs = refs[: count * fold], refs[count * fold]
    give, keep, total, high, low = refs[count * fold + 1 :]
    r, q, b = place(fold)
    assemble(chunks, high, low, fold, q, b)
    own_rows, own_cols = coeffs.shape
    less_one = coeffs[...] - identity((q * fold + b) * own_cols - r * own_rows, coeffs.shape)
    total[...] = dot3((high[...], low[...]), split(less_one), 0, 0)
    half = give.shape[0]
    mine = r & 1
    give[...] = total[rows_at((1 - mine) * half, half)]
    keep[...] = total[rows_at(mine * half, half)]


def halve_kernel(bit, fold, old_ref, got_ref, give, keep, total):
    r, _, _ = place(fold)
    total[...] = old_ref[...] + got_ref[...]
    half = give.shape[0]
    mine = lax.rem(lax.div(r, bit), 2)
    give[...] = total[rows_at((1 - mine) * half, half)]
    keep[...] = total[rows_at(mine * half, half)]


def share_kernel(fold, old_ref, got_ref, *refs):
    outs, total = refs[:-1], refs[-1]
    _, _, b = place(fold)
    total[...] = old_ref[...] + got_ref[...]
    width = outs[0].shape[0]
    for d in range(fold):
        outs[d][...] = total[rows_at((b ^ d) * width, width)]


def finish_kernel(fold, *refs):
    parts, out = refs[:fold], refs[fold]
    _, _, b = place(fold)
    cols = parts[0].shape[1]
    for e in range(fold):
        value = parts[0][...]
        for d in range(1, fold):
            value = jnp.where((b ^ e) == d, parts[d][...], value)
        out[:, e * cols : (e + 1) * cols] = value


def coeff_kernel(count, fold, *refs):
    coeffs, factors, col_factors = refs[:3]
    blocks, mirrored = refs[3 : 3 + count], refs[3 + count : 3 + count + fold]
    chunks, (out, high, low) = refs[3 + count + fold : -3], refs[-3:]
    r, q, b = place(fold)
    assemble(chunks, high, low, fold, q, b)
    features = blocks[0][...]
    for t in range(1, count):
        features = jnp.where((r ^ q) == t, blocks[t][...], features)
    features = split(features)
    right = split(col_factors[...])
    rows = mirrored[0].shape[0]
    for e in range(fold):
        at = slice(e * rows, (e + 1) * rows)
        turned = mirrored[0][...]
        for d in range(1, fold):
            turned = jnp.where((b ^ e) == d, mirrored[d][...], turned)
        turned = turned.T
        own = coeffs[at]
        symmetric = 0.5 * (own * own + turned * turned)
        relation = symmetric - dot3(split(factors[at]), right, 1, 1)
        outer = dot3((high[at], low[at]), features, 1, 1)
        out[at] = outer + 2.0 * own * relation


def per_device(coeffs, features, factors):
    row_count = lax.axis_size("row")
    col_count = lax.axis_size("col")
    fold = col_count // row_count
    own_rows, own_cols = coeffs.shape
    width = features.shape[1]
    quarter = own_rows // row_count
    piece = quarter // fold
    bits = [1 << n for n in range(row_count.bit_length() - 1)]
    every, both = range(row_count), range(fold)

    def send(value, route):
        pairs = []
        for i in every:
            for j in every:
                for k in both:
                    to = route(i, j, k)
                    if to is not None:
                        start = i * col_count + j * fold + k
                        pairs.append((start, to[0] * col_count + to[1] * fold + to[2]))
        return lax.ppermute(value, AXES, pairs)

    b = lax.axis_index("col") % fold
    blocks = {0: lax.dynamic_slice_in_dim(features, b * own_cols, own_cols, 0)}
    for bit in reversed(bits):
        for t in list(blocks):
            blocks[t | bit] = send(blocks[t], lambda i, j, k: (i ^ bit, j, k))
    blocks = [blocks[t] for t in every]

    cuts = [(0, quarter, lambda r, q, b, s=s: q ^ s) for s in every]
    cuts += [(0, own_cols, lambda r, q, b, d=d: b ^ d) for d in both]
    cuts += [(1, own_cols, lambda r, q, b: b)]
    cut = cut_rows([coeffs, factors], cuts, fold)
    parts, turns, col_factors = cut[:row_count], cut[row_count:-1], cut[-1]
    parts = [send(parts[s], lambda i, j, k: (i, j ^ s, k)) if s else parts[s] for s in every]

    def mirror(d, *deps):
        return send(after(turns[d], *deps), lambda i, j, k: (j, i, k ^ d))

    mirrored = {fold - 1: mirror(fold - 1, *parts)}

    shares = call(
        functools.partial(residual_kernel, row_count, fold),
        [shape(piece, width)] * fold,
        [*parts, *blocks],
        scratch=[pltpu.VMEM((quarter, width), F32)],
        flops=6 * quarter * row_count * own_cols * width,
        grant=12,
    )
    share = shares[0]
    for d in range(1, fold):
        got = send(shares[d], lambda i, j, k: (i, j, k ^ d))
        share = call(add_kernel, [shape(piece, width)], [share, got])[0]

    col_factors = after(col_factors, blocks[bits[-1]])
    for bit in reversed(bits):
        got = send(
            col_factors, lambda i, j, k: (i ^ bit, j, k) if (i ^ j) & (2 * bit - 1) == 0 else None
        )
        picked = functools.partial(pick_kernel, bit, fold)
        col_factors = call(picked, [shape(*got.shape)], [col_factors, got])[0]

    chunks = [send(share, lambda i, j, k: (i, j ^ s, k)) if s else share for s in every]
    spread = []
    for s in every:
        for d in both:
            one = chunks[s]
            spread.append(send(one, lambda i, j, k: (i, j, k ^ d)) if d else one)
    for d in range(fold - 1):
        mirrored[d] = mirror(d, *chunks)

    halves = [pltpu.VMEM((own_rows, width), BF16)] * 2
    give, keep = call(
        functools.partial(project_kernel, row_count, fold),
        [shape(width // 2, own_cols)] * 2,
        [*spread, coeffs],
        scratch=[pltpu.VMEM((width, own_cols), F32), *halves],
        flops=6 * own_rows * own_cols * width,
        grant=12,
    )
    for bit in bits:
        got = send(give, lambda i, j, k: (i ^ bit, j, k))
        rows = got.shape[0]
        total = pltpu.VMEM((rows, own_cols), F32)
        if bit != bits[-1]:
            give, keep = call(
                functools.partial(halve_kernel, 2 * bit, fold),
                [shape(rows // 2, own_cols)] * 2,
                [keep, got],
                scratch=[total],
            )
    pieces = call(
        functools.partial(share_kernel, fold),
        [shape(rows // fold, own_cols)] * fold,
        [keep, got],
        scratch=[total],
    )

    def turned(i):
        out = 0
        for bit in bits:
            out = 2 * out + (i // bit) % 2
        return out

    placed = [send(pieces[d], lambda i, j, k: (j, turned(i), k ^ d)) for d in both]
    grad_features = call(
        functools.partial(finish_kernel, fold), [shape(rows // fold, own_rows)], placed
    )[0].T

    grad_coeffs = call(
        functools.partial(coeff_kernel, row_count, fold),
        [shape(own_rows, own_cols)],
        [coeffs, factors, col_factors, *blocks, *[mirrored[d] for d in both], *spread],
        scratch=halves,
        flops=6 * own_rows * own_cols * (width + factors.shape[1]),
        grant=12,
    )[0]
    return (grad_coeffs, grad_features)


def solution(mesh):
    in_specs = (P("row", "col"), P("row", None), P("row", None))
    out_specs = (P("row", "col"), P("row", "col"))
    return jax.shard_map(
        per_device, mesh=mesh, in_specs=in_specs, out_specs=out_specs, check_vma=False
    )
```

```python
import functools
import jax
import jax.numpy as jnp
from jax import lax
from jax.experimental import pallas as pl
from jax.experimental.pallas import tpu as pltpu
from jax.sharding import PartitionSpec as P


AXES = ("row", "col")
F32, BF16 = jnp.float32, jnp.bfloat16


def after(value, *others):
    return lax.optimization_barrier((value, *others))[0]


def split(value):
    high = value.astype(BF16)
    return high, (value - high.astype(F32)).astype(BF16)


def dot3(left, right, left_dim, right_dim):
    def one(a, b):
        return lax.dot_general(
            a, b, (((left_dim,), (right_dim,)), ((), ())), preferred_element_type=F32
        )

    return one(left[0], right[0]) + (one(left[0], right[1]) + one(left[1], right[0]))


def place(fold):
    col = lax.axis_index("col")
    return lax.axis_index("row"), lax.div(col, fold), lax.rem(col, fold)


def identity(first, shape):
    rows = lax.broadcasted_iota(jnp.int32, shape, 0)
    cols = lax.broadcasted_iota(jnp.int32, shape, 1)
    return jnp.where(rows - cols == first, 1.0, 0.0)


def rows_at(start, count):
    return pl.ds(pl.multiple_of(start, count), count)


def call(kernel, outs, args, scratch=(), flops=0, hbm=(), grant=2):
    moved = sum(4 * a.size for a in args) + sum(4 * o.size for o in outs)
    spaces = [pltpu.HBM if n in hbm else pltpu.VMEM for n in range(len(args))]
    return pl.pallas_call(
        kernel,
        out_shape=outs,
        in_specs=[pl.BlockSpec(memory_space=space) for space in spaces],
        out_specs=[pl.BlockSpec(memory_space=pltpu.VMEM) for _ in outs],
        scratch_shapes=list(scratch),
        compiler_params=pltpu.CompilerParams(vmem_limit_bytes=grant << 20),
        cost_estimate=pl.CostEstimate(flops=flops, bytes_accessed=moved, transcendentals=0),
    )(*args)


def shape(*dims, dtype=F32):
    return jax.ShapeDtypeStruct(dims, dtype)


def cut_kernel(cuts, fold, *refs):
    count = max(cut[0] for cut in cuts) + 1
    ins, outs, sems = refs[:count], refs[count:-1], refs[-1]
    r, q, b = place(fold)
    copies = []
    for n, (source, rows, block) in enumerate(cuts):
        copies.append(
            pltpu.make_async_copy(
                ins[source].at[rows_at(block(r, q, b) * rows, rows)], outs[n], sems.at[n]
            )
        )
    for copy in copies:
        copy.start()
    for copy in copies:
        copy.wait()


def cut_rows(arrays, cuts, fold, grant):
    outs = [shape(rows, arrays[source].shape[1]) for source, rows, _ in cuts]
    return call(
        functools.partial(cut_kernel, cuts, fold),
        outs,
        arrays,
        scratch=[pltpu.SemaphoreType.DMA((len(cuts),))],
        hbm=range(len(arrays)),
        grant=grant,
    )


def residual_kernel(count, fold, *refs):
    parts, blocks, outs, total = refs[:count], refs[count : 2 * count], refs[2 * count : -1], refs[-1]
    r, q, b = place(fold)
    quarter, own_cols = parts[0].shape
    piece = quarter // fold
    for t in range(count):
        wanted = q ^ r ^ t
        left = parts[0][...]
        for s in range(1, count):
            left = jnp.where(wanted == s, parts[s][...], left)
        if t == 0:
            left = left - identity(b * own_cols - q * quarter, left.shape)
        product = dot3(split(left), split(blocks[t][...]), 1, 0)
        if t == 0:
            total[...] = product
        else:
            total[...] += product
    for d in range(fold):
        outs[d][...] = total[rows_at((b ^ d) * piece, piece)]


def assemble(chunks, high, low, fold, q, b):
    piece = chunks[0].shape[0]
    for n, chunk in enumerate(chunks):
        at = rows_at(((q ^ (n // fold)) * fold + (b ^ (n % fold))) * piece, piece)
        high[at], low[at] = split(chunk[...])


def add_kernel(left, right, out):
    out[...] = left[...] + right[...]


def pick_kernel(bit, fold, old_ref, got_ref, out):
    r, q, _ = place(fold)
    out[...] = jnp.where(((r ^ q) & (2 * bit - 1)) == bit, got_ref[...], old_ref[...])


def project_kernel(count, fold, *refs):
    chunks, coeffs = refs[: count * fold], refs[count * fold]
    give, keep, total, high, low = refs[count * fold + 1 :]
    r, q, b = place(fold)
    assemble(chunks, high, low, fold, q, b)
    own_rows, own_cols = coeffs.shape
    less_one = coeffs[...] - identity((q * fold + b) * own_cols - r * own_rows, coeffs.shape)
    total[...] = dot3((high[...], low[...]), split(less_one), 0, 0)
    half = give.shape[0]
    mine = r & 1
    give[...] = total[rows_at((1 - mine) * half, half)]
    keep[...] = total[rows_at(mine * half, half)]


def halve_kernel(bit, fold, old_ref, got_ref, give, keep, total):
    r, _, _ = place(fold)
    total[...] = old_ref[...] + got_ref[...]
    half = give.shape[0]
    mine = lax.rem(lax.div(r, bit), 2)
    give[...] = total[rows_at((1 - mine) * half, half)]
    keep[...] = total[rows_at(mine * half, half)]


def share_kernel(fold, old_ref, got_ref, *refs):
    outs, total = refs[:-1], refs[-1]
    _, _, b = place(fold)
    total[...] = old_ref[...] + got_ref[...]
    width = outs[0].shape[0]
    for d in range(fold):
        outs[d][...] = total[rows_at((b ^ d) * width, width)]


def finish_kernel(fold, *refs):
    parts, out = refs[:fold], refs[fold]
    _, _, b = place(fold)
    cols = parts[0].shape[1]
    for e in range(fold):
        value = parts[0][...]
        for d in range(1, fold):
            value = jnp.where((b ^ e) == d, parts[d][...], value)
        out[:, e * cols : (e + 1) * cols] = value


def coeff_kernel(count, fold, *refs):
    coeffs, factors, col_factors = refs[:3]
    blocks, mirrored = refs[3 : 3 + count], refs[3 + count : 3 + count + fold]
    chunks, (out, high, low) = refs[3 + count + fold : -3], refs[-3:]
    r, q, b = place(fold)
    assemble(chunks, high, low, fold, q, b)
    features = blocks[0][...]
    for t in range(1, count):
        features = jnp.where((r ^ q) == t, blocks[t][...], features)
    features = split(features)
    right = split(col_factors[...])
    rows = mirrored[0].shape[0]
    for e in range(fold):
        at = slice(e * rows, (e + 1) * rows)
        turned = mirrored[0][...]
        for d in range(1, fold):
            turned = jnp.where((b ^ e) == d, mirrored[d][...], turned)
        turned = turned.T
        own = coeffs[at]
        symmetric = 0.5 * (own * own + turned * turned)
        relation = symmetric - dot3(split(factors[at]), right, 1, 1)
        outer = dot3((high[at], low[at]), features, 1, 1)
        out[at] = outer + 2.0 * own * relation


def per_device(coeffs, features, factors):
    row_count = lax.axis_size("row")
    col_count = lax.axis_size("col")
    fold = col_count // row_count
    own_rows, own_cols = coeffs.shape
    width = features.shape[1]
    quarter = own_rows // row_count
    piece = quarter // fold
    bits = [1 << n for n in range(row_count.bit_length() - 1)]
    every, both = range(row_count), range(fold)

    def send(value, route):
        pairs = []
        for i in every:
            for j in every:
                for k in both:
                    to = route(i, j, k)
                    if to is not None:
                        start = i * col_count + j * fold + k
                        pairs.append((start, to[0] * col_count + to[1] * fold + to[2]))
        return lax.ppermute(value, AXES, pairs)

    cuts = [(0, own_cols, lambda r, q, b: b)]
    blocks = {0: cut_rows([features], cuts, fold, 63)[0]}
    for bit in reversed(bits):
        for t in list(blocks):
            blocks[t | bit] = send(blocks[t], lambda i, j, k: (i ^ bit, j, k))
    blocks = [blocks[t] for t in every]

    cuts = [(0, quarter, lambda r, q, b, s=s: q ^ s) for s in every]
    cuts += [(0, own_cols, lambda r, q, b, d=d: b ^ d) for d in both]
    cuts += [(1, own_cols, lambda r, q, b: b)]
    cut = cut_rows([coeffs, factors], cuts, fold, 2)
    parts, turns, col_factors = cut[:row_count], cut[row_count:-1], cut[-1]
    parts = [send(parts[s], lambda i, j, k: (i, j ^ s, k)) if s else parts[s] for s in every]

    turns = [send(turns[d], lambda i, j, k: (i, j, k ^ d)) if d else turns[d] for d in both]

    def mirror(d, *deps):
        return send(after(turns[d], *deps), lambda i, j, k: (j, i, k))

    mirrored = {0: mirror(0, *parts)}

    shares = call(
        functools.partial(residual_kernel, row_count, fold),
        [shape(piece, width)] * fold,
        [*parts, *blocks],
        scratch=[pltpu.VMEM((quarter, width), F32)],
        flops=6 * quarter * row_count * own_cols * width,
        grant=12,
    )
    share = shares[0]
    for d in range(1, fold):
        got = send(shares[d], lambda i, j, k: (i, j, k ^ d))
        share = call(add_kernel, [shape(piece, width)], [share, got])[0]

    col_factors = after(col_factors, blocks[bits[-1]])
    for bit in reversed(bits):
        got = send(
            col_factors, lambda i, j, k: (i ^ bit, j, k) if (i ^ j) & (2 * bit - 1) == 0 else None
        )
        picked = functools.partial(pick_kernel, bit, fold)
        col_factors = call(picked, [shape(*got.shape)], [col_factors, got])[0]

    chunks = [send(share, lambda i, j, k: (i, j ^ s, k)) if s else share for s in every]
    spread = []
    for s in every:
        for d in both:
            one = chunks[s]
            spread.append(send(one, lambda i, j, k: (i, j, k ^ d)) if d else one)
    for d in range(1, fold):
        mirrored[d] = mirror(d, *chunks)

    halves = [pltpu.VMEM((own_rows, width), BF16)] * 2
    give, keep = call(
        functools.partial(project_kernel, row_count, fold),
        [shape(width // 2, own_cols)] * 2,
        [*spread, coeffs],
        scratch=[pltpu.VMEM((width, own_cols), F32), *halves],
        flops=6 * own_rows * own_cols * width,
        grant=12,
    )
    for bit in bits:
        got = send(give, lambda i, j, k: (i ^ bit, j, k))
        rows = got.shape[0]
        total = pltpu.VMEM((rows, own_cols), F32)
        if bit != bits[-1]:
            give, keep = call(
                functools.partial(halve_kernel, 2 * bit, fold),
                [shape(rows // 2, own_cols)] * 2,
                [keep, got],
                scratch=[total],
            )
    pieces = call(
        functools.partial(share_kernel, fold),
        [shape(rows // fold, own_cols)] * fold,
        [keep, got],
        scratch=[total],
    )

    def turned(i):
        out = 0
        for bit in bits:
            out = 2 * out + (i // bit) % 2
        return out

    placed = [send(pieces[d], lambda i, j, k: (j, turned(i), k ^ d)) for d in both]
    grad_features = call(
        functools.partial(finish_kernel, fold), [shape(rows // fold, own_rows)], placed
    )[0].T

    grad_coeffs = call(
        functools.partial(coeff_kernel, row_count, fold),
        [shape(own_rows, own_cols)],
        [coeffs, factors, col_factors, *blocks, *[mirrored[d] for d in both], *spread],
        scratch=halves,
        flops=6 * own_rows * own_cols * (width + factors.shape[1]),
        grant=12,
    )[0]
    return (grad_coeffs, grad_features)


def solution(mesh):
    in_specs = (P("row", "col"), P("row", None), P("row", None))
    out_specs = (P("row", "col"), P("row", "col"))
    return jax.shard_map(
        per_device, mesh=mesh, in_specs=in_specs, out_specs=out_specs, check_vma=False
    )
```

```python
import functools
import jax
import jax.numpy as jnp
from jax import lax
from jax.experimental import pallas as pl
from jax.experimental.pallas import tpu as pltpu
from jax.sharding import PartitionSpec as P


AXES = ("row", "col")
F32, BF16 = jnp.float32, jnp.bfloat16


def after(value, *others):
    return lax.optimization_barrier((value, *others))[0]


def split(value):
    high = value.astype(BF16)
    return high, (value - high.astype(F32)).astype(BF16)


def dot3(left, right, left_dim, right_dim):
    def one(a, b):
        return lax.dot_general(
            a, b, (((left_dim,), (right_dim,)), ((), ())), preferred_element_type=F32
        )

    return one(left[0], right[0]) + (one(left[0], right[1]) + one(left[1], right[0]))


def place(fold):
    col = lax.axis_index("col")
    return lax.axis_index("row"), lax.div(col, fold), lax.rem(col, fold)


def identity(first, shape):
    rows = lax.broadcasted_iota(jnp.int32, shape, 0)
    cols = lax.broadcasted_iota(jnp.int32, shape, 1)
    return jnp.where(rows - cols == first, 1.0, 0.0)


def rows_at(start, count):
    return pl.ds(pl.multiple_of(start, count), count)


def call(kernel, outs, args, scratch=(), flops=0, hbm=(), grant=2):
    moved = sum(4 * a.size for a in args) + sum(4 * o.size for o in outs)
    spaces = [pltpu.HBM if n in hbm else pltpu.VMEM for n in range(len(args))]
    return pl.pallas_call(
        kernel,
        out_shape=outs,
        in_specs=[pl.BlockSpec(memory_space=space) for space in spaces],
        out_specs=[pl.BlockSpec(memory_space=pltpu.VMEM) for _ in outs],
        scratch_shapes=list(scratch),
        compiler_params=pltpu.CompilerParams(vmem_limit_bytes=grant << 20),
        cost_estimate=pl.CostEstimate(flops=flops, bytes_accessed=moved, transcendentals=0),
    )(*args)


def shape(*dims, dtype=F32):
    return jax.ShapeDtypeStruct(dims, dtype)


def cut_kernel(cuts, fold, *refs):
    count = max(cut[0] for cut in cuts) + 1
    ins, outs, sems = refs[:count], refs[count:-1], refs[-1]
    r, q, b = place(fold)
    copies = []
    for n, (source, rows, block) in enumerate(cuts):
        copies.append(
            pltpu.make_async_copy(
                ins[source].at[rows_at(block(r, q, b) * rows, rows)], outs[n], sems.at[n]
            )
        )
    for copy in copies:
        copy.start()
    for copy in copies:
        copy.wait()


def cut_rows(arrays, cuts, fold):
    outs = [shape(rows, arrays[source].shape[1]) for source, rows, _ in cuts]
    return call(
        functools.partial(cut_kernel, cuts, fold),
        outs,
        arrays,
        scratch=[pltpu.SemaphoreType.DMA((len(cuts),))],
        hbm=range(len(arrays)),
    )


def residual_kernel(count, fold, *refs):
    parts, blocks, outs, total = refs[:count], refs[count : 2 * count], refs[2 * count : -1], refs[-1]
    r, q, b = place(fold)
    quarter, own_cols = parts[0].shape
    piece = quarter // fold
    for t in range(count):
        wanted = q ^ r ^ t
        left = parts[0][...]
        for s in range(1, count):
            left = jnp.where(wanted == s, parts[s][...], left)
        if t == 0:
            left = left - identity(b * own_cols - q * quarter, left.shape)
        product = dot3(split(left), split(blocks[t][...]), 1, 0)
        if t == 0:
            total[...] = product
        else:
            total[...] += product
    for d in range(fold):
        outs[d][...] = total[rows_at((b ^ d) * piece, piece)]


def assemble(chunks, high, low, fold, q, b):
    piece = chunks[0].shape[0]
    for n, chunk in enumerate(chunks):
        at = rows_at(((q ^ (n // fold)) * fold + (b ^ (n % fold))) * piece, piece)
        high[at], low[at] = split(chunk[...])


def add_kernel(left, right, out):
    out[...] = left[...] + right[...]


def pick_kernel(bit, fold, old_ref, got_ref, out):
    r, q, _ = place(fold)
    out[...] = jnp.where(((r ^ q) & (2 * bit - 1)) == bit, got_ref[...], old_ref[...])


def project_kernel(count, fold, *refs):
    chunks, coeffs = refs[: count * fold], refs[count * fold]
    give, keep, total, high, low = refs[count * fold + 1 :]
    r, q, b = place(fold)
    assemble(chunks, high, low, fold, q, b)
    own_rows, own_cols = coeffs.shape
    less_one = coeffs[...] - identity((q * fold + b) * own_cols - r * own_rows, coeffs.shape)
    total[...] = dot3((high[...], low[...]), split(less_one), 0, 0)
    half = give.shape[0]
    mine = r & 1
    give[...] = total[rows_at((1 - mine) * half, half)]
    keep[...] = total[rows_at(mine * half, half)]


def halve_kernel(bit, fold, old_ref, got_ref, give, keep, total):
    r, _, _ = place(fold)
    total[...] = old_ref[...] + got_ref[...]
    half = give.shape[0]
    mine = lax.rem(lax.div(r, bit), 2)
    give[...] = total[rows_at((1 - mine) * half, half)]
    keep[...] = total[rows_at(mine * half, half)]


def share_kernel(fold, old_ref, got_ref, *refs):
    outs, total = refs[:-1], refs[-1]
    _, _, b = place(fold)
    total[...] = old_ref[...] + got_ref[...]
    width = outs[0].shape[0]
    for d in range(fold):
        outs[d][...] = total[rows_at((b ^ d) * width, width)]


def finish_kernel(fold, *refs):
    parts, out = refs[:fold], refs[fold]
    _, _, b = place(fold)
    cols = parts[0].shape[1]
    for e in range(fold):
        value = parts[0][...]
        for d in range(1, fold):
            value = jnp.where((b ^ e) == d, parts[d][...], value)
        out[:, e * cols : (e + 1) * cols] = value


def coeff_kernel(count, fold, *refs):
    coeffs, factors, col_factors = refs[:3]
    blocks, mirrored = refs[3 : 3 + count], refs[3 + count : 3 + count + fold]
    chunks, (out, high, low) = refs[3 + count + fold : -3], refs[-3:]
    r, q, b = place(fold)
    assemble(chunks, high, low, fold, q, b)
    features = blocks[0][...]
    for t in range(1, count):
        features = jnp.where((r ^ q) == t, blocks[t][...], features)
    features = split(features)
    right = split(col_factors[...])
    rows = mirrored[0].shape[0]
    for e in range(fold):
        at = slice(e * rows, (e + 1) * rows)
        turned = mirrored[0][...]
        for d in range(1, fold):
            turned = jnp.where((b ^ e) == d, mirrored[d][...], turned)
        turned = turned.T
        own = coeffs[at]
        symmetric = 0.5 * (own * own + turned * turned)
        relation = symmetric - dot3(split(factors[at]), right, 1, 1)
        outer = dot3((high[at], low[at]), features, 1, 1)
        out[at] = outer + 2.0 * own * relation


def per_device(coeffs, features, factors):
    row_count = lax.axis_size("row")
    col_count = lax.axis_size("col")
    fold = col_count // row_count
    own_rows, own_cols = coeffs.shape
    width = features.shape[1]
    quarter = own_rows // row_count
    piece = quarter // fold
    bits = [1 << n for n in range(row_count.bit_length() - 1)]
    every, both = range(row_count), range(fold)

    def send(value, route):
        pairs = []
        for i in every:
            for j in every:
                for k in both:
                    to = route(i, j, k)
                    if to is not None:
                        start = i * col_count + j * fold + k
                        pairs.append((start, to[0] * col_count + to[1] * fold + to[2]))
        return lax.ppermute(value, AXES, pairs)

    b = lax.axis_index("col") % fold
    blocks = {0: lax.dynamic_slice_in_dim(features, b * own_cols, own_cols, 0)}
    for bit in reversed(bits):
        for t in list(blocks):
            blocks[t | bit] = send(blocks[t], lambda i, j, k: (i ^ bit, j, k))
    blocks = [blocks[t] for t in every]

    cuts = [(0, quarter, lambda r, q, b, s=s: q ^ s) for s in every]
    cuts += [(0, own_cols, lambda r, q, b, d=d: b ^ d) for d in both]
    cuts += [(1, own_cols, lambda r, q, b: b)]
    cut = cut_rows([coeffs, factors], cuts, fold)
    parts, turns, col_factors = cut[:row_count], cut[row_count:-1], cut[-1]
    parts = [send(parts[s], lambda i, j, k: (i, j ^ s, k)) if s else parts[s] for s in every]

    turns = [send(turns[d], lambda i, j, k: (i, j, k ^ d)) if d else turns[d] for d in both]

    def mirror(d, *deps):
        return send(after(turns[d], *deps), lambda i, j, k: (j, i, k))

    mirrored = {0: mirror(0)}

    shares = call(
        functools.partial(residual_kernel, row_count, fold),
        [shape(piece, width)] * fold,
        [*parts, *blocks],
        scratch=[pltpu.VMEM((quarter, width), F32)],
        flops=6 * quarter * row_count * own_cols * width,
        grant=12,
    )
    share = shares[0]
    for d in range(1, fold):
        got = send(shares[d], lambda i, j, k: (i, j, k ^ d))
        share = call(add_kernel, [shape(piece, width)], [share, got])[0]

    for bit in reversed(bits):
        got = send(
            col_factors, lambda i, j, k: (i ^ bit, j, k) if (i ^ j) & (2 * bit - 1) == 0 else None
        )
        picked = functools.partial(pick_kernel, bit, fold)
        col_factors = call(picked, [shape(*got.shape)], [col_factors, got])[0]

    chunks = [send(share, lambda i, j, k: (i, j ^ s, k)) if s else share for s in every]
    spread = []
    for s in every:
        for d in both:
            one = chunks[s]
            spread.append(send(one, lambda i, j, k: (i, j, k ^ d)) if d else one)
    for d in range(1, fold):
        mirrored[d] = mirror(d, *chunks)

    halves = [pltpu.VMEM((own_rows, width), BF16)] * 2
    give, keep = call(
        functools.partial(project_kernel, row_count, fold),
        [shape(width // 2, own_cols)] * 2,
        [*spread, coeffs],
        scratch=[pltpu.VMEM((width, own_cols), F32), *halves],
        flops=6 * own_rows * own_cols * width,
        grant=12,
    )
    for bit in bits:
        got = send(give, lambda i, j, k: (i ^ bit, j, k))
        rows = got.shape[0]
        total = pltpu.VMEM((rows, own_cols), F32)
        if bit != bits[-1]:
            give, keep = call(
                functools.partial(halve_kernel, 2 * bit, fold),
                [shape(rows // 2, own_cols)] * 2,
                [keep, got],
                scratch=[total],
            )
    pieces = call(
        functools.partial(share_kernel, fold),
        [shape(rows // fold, own_cols)] * fold,
        [keep, got],
        scratch=[total],
    )

    def turned(i):
        out = 0
        for bit in bits:
            out = 2 * out + (i // bit) % 2
        return out

    placed = [send(pieces[d], lambda i, j, k: (j, turned(i), k ^ d)) for d in both]
    grad_features = call(
        functools.partial(finish_kernel, fold), [shape(rows // fold, own_rows)], placed
    )[0].T

    grad_coeffs = call(
        functools.partial(coeff_kernel, row_count, fold),
        [shape(own_rows, own_cols)],
        [coeffs, factors, col_factors, *blocks, *[mirrored[d] for d in both], *spread],
        scratch=halves,
        flops=6 * own_rows * own_cols * (width + factors.shape[1]),
        grant=12,
    )[0]
    return (grad_coeffs, grad_features)


def solution(mesh):
    in_specs = (P("row", "col"), P("row", None), P("row", None))
    out_specs = (P("row", "col"), P("row", "col"))
    return jax.shard_map(
        per_device, mesh=mesh, in_specs=in_specs, out_specs=out_specs, check_vma=False
    )
```

```python
import functools
import jax
import jax.numpy as jnp
from jax import lax
from jax.experimental import pallas as pl
from jax.experimental.pallas import tpu as pltpu
from jax.sharding import PartitionSpec as P


AXES = ("row", "col")
F32, BF16 = jnp.float32, jnp.bfloat16


def after(value, *others):
    return lax.optimization_barrier((value, *others))[0]


def split(value):
    high = value.astype(BF16)
    return high, (value - high.astype(F32)).astype(BF16)


def dot3(left, right, left_dim, right_dim):
    def one(a, b):
        return lax.dot_general(
            a, b, (((left_dim,), (right_dim,)), ((), ())), preferred_element_type=F32
        )

    return one(left[0], right[0]) + (one(left[0], right[1]) + one(left[1], right[0]))


def place(fold):
    col = lax.axis_index("col")
    return lax.axis_index("row"), lax.div(col, fold), lax.rem(col, fold)


def identity(first, shape):
    rows = lax.broadcasted_iota(jnp.int32, shape, 0)
    cols = lax.broadcasted_iota(jnp.int32, shape, 1)
    return jnp.where(rows - cols == first, 1.0, 0.0)


def rows_at(start, count):
    return pl.ds(pl.multiple_of(start, count), count)


def call(kernel, outs, args, scratch=(), flops=0, hbm=(), grant=2):
    moved = sum(4 * a.size for a in args) + sum(4 * o.size for o in outs)
    spaces = [pltpu.HBM if n in hbm else pltpu.VMEM for n in range(len(args))]
    return pl.pallas_call(
        kernel,
        out_shape=outs,
        in_specs=[pl.BlockSpec(memory_space=space) for space in spaces],
        out_specs=[pl.BlockSpec(memory_space=pltpu.VMEM) for _ in outs],
        scratch_shapes=list(scratch),
        compiler_params=pltpu.CompilerParams(vmem_limit_bytes=grant << 20),
        cost_estimate=pl.CostEstimate(flops=flops, bytes_accessed=moved, transcendentals=0),
    )(*args)


def shape(*dims, dtype=F32):
    return jax.ShapeDtypeStruct(dims, dtype)


def cut_kernel(cuts, fold, *refs):
    count = max(cut[0] for cut in cuts) + 1
    ins, outs, sems = refs[:count], refs[count:-1], refs[-1]
    r, q, b = place(fold)
    copies = []
    for n, (source, rows, block) in enumerate(cuts):
        copies.append(
            pltpu.make_async_copy(
                ins[source].at[rows_at(block(r, q, b) * rows, rows)], outs[n], sems.at[n]
            )
        )
    for copy in copies:
        copy.start()
    for copy in copies:
        copy.wait()


def cut_rows(arrays, cuts, fold):
    outs = [shape(rows, arrays[source].shape[1]) for source, rows, _ in cuts]
    return call(
        functools.partial(cut_kernel, cuts, fold),
        outs,
        arrays,
        scratch=[pltpu.SemaphoreType.DMA((len(cuts),))],
        hbm=range(len(arrays)),
    )


def residual_kernel(count, fold, *refs):
    parts, blocks, outs, total = refs[:count], refs[count : 2 * count], refs[2 * count : -1], refs[-1]
    r, q, b = place(fold)
    quarter, own_cols = parts[0].shape
    piece = quarter // fold
    for t in range(count):
        wanted = q ^ r ^ t
        left = parts[0][...]
        for s in range(1, count):
            left = jnp.where(wanted == s, parts[s][...], left)
        if t == 0:
            left = left - identity(b * own_cols - q * quarter, left.shape)
        product = dot3(split(left), split(blocks[t][...]), 1, 0)
        if t == 0:
            total[...] = product
        else:
            total[...] += product
    for d in range(fold):
        outs[d][...] = total[rows_at((b ^ d) * piece, piece)]


def assemble(chunks, high, low, fold, q, b):
    piece = chunks[0].shape[0]
    for n, chunk in enumerate(chunks):
        at = rows_at(((q ^ (n // fold)) * fold + (b ^ (n % fold))) * piece, piece)
        high[at], low[at] = split(chunk[...])


def add_kernel(left, right, out):
    out[...] = left[...] + right[...]


def pick_kernel(bit, fold, old_ref, got_ref, out):
    r, q, _ = place(fold)
    out[...] = jnp.where(((r ^ q) & (2 * bit - 1)) == bit, got_ref[...], old_ref[...])


def project_kernel(count, fold, *refs):
    chunks, coeffs = refs[: count * fold], refs[count * fold]
    give, keep, total, high, low = refs[count * fold + 1 :]
    r, q, b = place(fold)
    assemble(chunks, high, low, fold, q, b)
    own_rows, own_cols = coeffs.shape
    less_one = coeffs[...] - identity((q * fold + b) * own_cols - r * own_rows, coeffs.shape)
    total[...] = dot3((high[...], low[...]), split(less_one), 0, 0)
    half = give.shape[0]
    mine = r & 1
    give[...] = total[rows_at((1 - mine) * half, half)]
    keep[...] = total[rows_at(mine * half, half)]


def halve_kernel(bit, fold, old_ref, got_ref, give, keep, total):
    r, _, _ = place(fold)
    total[...] = old_ref[...] + got_ref[...]
    half = give.shape[0]
    mine = lax.rem(lax.div(r, bit), 2)
    give[...] = total[rows_at((1 - mine) * half, half)]
    keep[...] = total[rows_at(mine * half, half)]


def share_kernel(fold, old_ref, got_ref, *refs):
    outs, total = refs[:-1], refs[-1]
    _, _, b = place(fold)
    total[...] = old_ref[...] + got_ref[...]
    width = outs[0].shape[0]
    for d in range(fold):
        outs[d][...] = total[rows_at((b ^ d) * width, width)]


def finish_kernel(fold, *refs):
    parts, out = refs[:fold], refs[fold]
    _, _, b = place(fold)
    cols = parts[0].shape[1]
    for e in range(fold):
        value = parts[0][...]
        for d in range(1, fold):
            value = jnp.where((b ^ e) == d, parts[d][...], value)
        out[:, e * cols : (e + 1) * cols] = value


def coeff_kernel(count, fold, *refs):
    coeffs, factors, col_factors = refs[:3]
    blocks, mirrored = refs[3 : 3 + count], refs[3 + count : 3 + count + fold]
    chunks, (out, high, low) = refs[3 + count + fold : -3], refs[-3:]
    r, q, b = place(fold)
    assemble(chunks, high, low, fold, q, b)
    features = blocks[0][...]
    for t in range(1, count):
        features = jnp.where((r ^ q) == t, blocks[t][...], features)
    features = split(features)
    right = split(col_factors[...])
    rows = mirrored[0].shape[0]
    for e in range(fold):
        at = slice(e * rows, (e + 1) * rows)
        turned = mirrored[0][...]
        for d in range(1, fold):
            turned = jnp.where((b ^ e) == d, mirrored[d][...], turned)
        turned = turned.T
        own = coeffs[at]
        symmetric = 0.5 * (own * own + turned * turned)
        relation = symmetric - dot3(split(factors[at]), right, 1, 1)
        outer = dot3((high[at], low[at]), features, 1, 1)
        out[at] = outer + 2.0 * own * relation


def per_device(coeffs, features, factors):
    row_count = lax.axis_size("row")
    col_count = lax.axis_size("col")
    fold = col_count // row_count
    own_rows, own_cols = coeffs.shape
    width = features.shape[1]
    quarter = own_rows // row_count
    piece = quarter // fold
    bits = [1 << n for n in range(row_count.bit_length() - 1)]
    every, both = range(row_count), range(fold)

    def send(value, route):
        pairs = []
        for i in every:
            for j in every:
                for k in both:
                    to = route(i, j, k)
                    if to is not None:
                        start = i * col_count + j * fold + k
                        pairs.append((start, to[0] * col_count + to[1] * fold + to[2]))
        return lax.ppermute(value, AXES, pairs)

    b = lax.axis_index("col") % fold
    blocks = {0: lax.dynamic_slice_in_dim(features, b * own_cols, own_cols, 0)}
    for bit in reversed(bits):
        for t in list(blocks):
            blocks[t | bit] = send(blocks[t], lambda i, j, k: (i ^ bit, j, k))
    blocks = [blocks[t] for t in every]

    cuts = [(0, quarter, lambda r, q, b, s=s: q ^ s) for s in every]
    cuts += [(0, own_cols, lambda r, q, b, d=d: b ^ d) for d in both]
    cuts += [(1, own_cols, lambda r, q, b: b)]
    cut = cut_rows([coeffs, factors], cuts, fold)
    parts, turns, col_factors = cut[:row_count], cut[row_count:-1], cut[-1]
    parts = [send(parts[s], lambda i, j, k: (i, j ^ s, k)) if s else parts[s] for s in every]

    turns = [send(turns[d], lambda i, j, k: (i, j, k ^ d)) if d else turns[d] for d in both]

    def mirror(d, *deps):
        return send(after(turns[d], *deps), lambda i, j, k: (j, i, k))

    mirrored = {0: mirror(0)}

    shares = call(
        functools.partial(residual_kernel, row_count, fold),
        [shape(piece, width)] * fold,
        [*parts, *blocks],
        scratch=[pltpu.VMEM((quarter, width), F32)],
        flops=6 * quarter * row_count * own_cols * width,
        grant=12,
    )
    share = shares[0]
    for d in range(1, fold):
        got = send(shares[d], lambda i, j, k: (i, j, k ^ d))
        share = call(add_kernel, [shape(piece, width)], [share, got])[0]

    for bit in reversed(bits):
        got = send(
            col_factors, lambda i, j, k: (i ^ bit, j, k) if (i ^ j) & (2 * bit - 1) == 0 else None
        )
        picked = functools.partial(pick_kernel, bit, fold)
        col_factors = call(picked, [shape(*got.shape)], [col_factors, got])[0]

    chunks = {0: share}
    for bit in reversed(bits):
        for s in list(chunks):
            chunks[s | bit] = send(chunks[s], lambda i, j, k: (i, j ^ bit, k))
    chunks = [chunks[s] for s in every]
    spread = []
    for s in every:
        for d in both:
            one = chunks[s]
            spread.append(send(one, lambda i, j, k: (i, j, k ^ d)) if d else one)
    for d in range(1, fold):
        mirrored[d] = mirror(d, *chunks)

    halves = [pltpu.VMEM((own_rows, width), BF16)] * 2
    give, keep = call(
        functools.partial(project_kernel, row_count, fold),
        [shape(width // 2, own_cols)] * 2,
        [*spread, coeffs],
        scratch=[pltpu.VMEM((width, own_cols), F32), *halves],
        flops=6 * own_rows * own_cols * width,
        grant=12,
    )
    for bit in bits:
        got = send(give, lambda i, j, k: (i ^ bit, j, k))
        rows = got.shape[0]
        total = pltpu.VMEM((rows, own_cols), F32)
        if bit != bits[-1]:
            give, keep = call(
                functools.partial(halve_kernel, 2 * bit, fold),
                [shape(rows // 2, own_cols)] * 2,
                [keep, got],
                scratch=[total],
            )
    pieces = call(
        functools.partial(share_kernel, fold),
        [shape(rows // fold, own_cols)] * fold,
        [keep, got],
        scratch=[total],
    )

    def turned(i):
        out = 0
        for bit in bits:
            out = 2 * out + (i // bit) % 2
        return out

    placed = [send(pieces[d], lambda i, j, k: (j, turned(i), k ^ d)) for d in both]
    grad_features = call(
        functools.partial(finish_kernel, fold), [shape(rows // fold, own_rows)], placed
    )[0].T

    grad_coeffs = call(
        functools.partial(coeff_kernel, row_count, fold),
        [shape(own_rows, own_cols)],
        [coeffs, factors, col_factors, *blocks, *[mirrored[d] for d in both], *spread],
        scratch=halves,
        flops=6 * own_rows * own_cols * (width + factors.shape[1]),
        grant=12,
    )[0]
    return (grad_coeffs, grad_features)


def solution(mesh):
    in_specs = (P("row", "col"), P("row", None), P("row", None))
    out_specs = (P("row", "col"), P("row", "col"))
    return jax.shard_map(
        per_device, mesh=mesh, in_specs=in_specs, out_specs=out_specs, check_vma=False
    )
```

```python
import functools
import jax
import jax.numpy as jnp
from jax import lax
from jax.experimental import pallas as pl
from jax.experimental.pallas import tpu as pltpu
from jax.sharding import PartitionSpec as P


AXES = ("row", "col")
F32, BF16 = jnp.float32, jnp.bfloat16


def split(value):
    high = value.astype(BF16)
    return high, (value - high.astype(F32)).astype(BF16)


def dot3(left, right, left_dim, right_dim):
    def one(a, b):
        return lax.dot_general(
            a, b, (((left_dim,), (right_dim,)), ((), ())), preferred_element_type=F32
        )

    return one(left[0], right[0]) + (one(left[0], right[1]) + one(left[1], right[0]))


def place(fold):
    col = lax.axis_index("col")
    return lax.axis_index("row"), lax.div(col, fold), lax.rem(col, fold)


def identity(first, shape):
    rows = lax.broadcasted_iota(jnp.int32, shape, 0)
    cols = lax.broadcasted_iota(jnp.int32, shape, 1)
    return jnp.where(rows - cols == first, 1.0, 0.0)


def rows_at(start, count):
    return pl.ds(pl.multiple_of(start, count), count)


def call(kernel, outs, args, scratch=(), flops=0, hbm=(), grant=2):
    moved = sum(4 * a.size for a in args) + sum(4 * o.size for o in outs)
    spaces = [pltpu.HBM if n in hbm else pltpu.VMEM for n in range(len(args))]
    return pl.pallas_call(
        kernel,
        out_shape=outs,
        in_specs=[pl.BlockSpec(memory_space=space) for space in spaces],
        out_specs=[pl.BlockSpec(memory_space=pltpu.VMEM) for _ in outs],
        scratch_shapes=list(scratch),
        compiler_params=pltpu.CompilerParams(vmem_limit_bytes=grant << 20),
        cost_estimate=pl.CostEstimate(flops=flops, bytes_accessed=moved, transcendentals=0),
    )(*args)


def shape(*dims, dtype=F32):
    return jax.ShapeDtypeStruct(dims, dtype)


def cut_kernel(cuts, fold, *refs):
    count = max(cut[0] for cut in cuts) + 1
    ins, outs, sems = refs[:count], refs[count:-1], refs[-1]
    r, q, b = place(fold)
    copies = []
    for n, (source, rows, block) in enumerate(cuts):
        copies.append(
            pltpu.make_async_copy(
                ins[source].at[rows_at(block(r, q, b) * rows, rows)], outs[n], sems.at[n]
            )
        )
    for copy in copies:
        copy.start()
    for copy in copies:
        copy.wait()


def cut_rows(arrays, cuts, fold):
    outs = [shape(rows, arrays[source].shape[1]) for source, rows, _ in cuts]
    return call(
        functools.partial(cut_kernel, cuts, fold),
        outs,
        arrays,
        scratch=[pltpu.SemaphoreType.DMA((len(cuts),))],
        hbm=range(len(arrays)),
    )


def residual_kernel(count, fold, *refs):
    parts, blocks, outs, total = refs[:count], refs[count : 2 * count], refs[2 * count : -1], refs[-1]
    r, q, b = place(fold)
    quarter, own_cols = parts[0].shape
    piece = quarter // fold
    for t in range(count):
        wanted = q ^ r ^ t
        left = parts[0][...]
        for s in range(1, count):
            left = jnp.where(wanted == s, parts[s][...], left)
        if t == 0:
            left = left - identity(b * own_cols - q * quarter, left.shape)
        product = dot3(split(left), split(blocks[t][...]), 1, 0)
        if t == 0:
            total[...] = product
        else:
            total[...] += product
    for d in range(fold):
        outs[d][...] = total[rows_at((b ^ d) * piece, piece)]


def assemble(chunks, high, low, fold, q, b):
    piece = chunks[0].shape[0]
    for n, chunk in enumerate(chunks):
        at = rows_at(((q ^ (n // fold)) * fold + (b ^ (n % fold))) * piece, piece)
        high[at], low[at] = split(chunk[...])


def add_kernel(left, right, out):
    out[...] = left[...] + right[...]


def pick_kernel(bit, fold, old_ref, got_ref, out):
    r, q, _ = place(fold)
    out[...] = jnp.where(((r ^ q) & (2 * bit - 1)) == bit, got_ref[...], old_ref[...])


def project_kernel(count, fold, *refs):
    chunks, coeffs = refs[: count * fold], refs[count * fold]
    give, keep, total, high, low = refs[count * fold + 1 :]
    r, q, b = place(fold)
    assemble(chunks, high, low, fold, q, b)
    own_rows, own_cols = coeffs.shape
    less_one = coeffs[...] - identity((q * fold + b) * own_cols - r * own_rows, coeffs.shape)
    total[...] = dot3((high[...], low[...]), split(less_one), 0, 0)
    half = give.shape[0]
    mine = r & 1
    give[...] = total[rows_at((1 - mine) * half, half)]
    keep[...] = total[rows_at(mine * half, half)]


def halve_kernel(bit, fold, old_ref, got_ref, give, keep, total):
    r, _, _ = place(fold)
    total[...] = old_ref[...] + got_ref[...]
    half = give.shape[0]
    mine = lax.rem(lax.div(r, bit), 2)
    give[...] = total[rows_at((1 - mine) * half, half)]
    keep[...] = total[rows_at(mine * half, half)]


def share_kernel(fold, old_ref, got_ref, *refs):
    outs, total = refs[:-1], refs[-1]
    _, _, b = place(fold)
    total[...] = old_ref[...] + got_ref[...]
    width = outs[0].shape[0]
    for d in range(fold):
        outs[d][...] = total[rows_at((b ^ d) * width, width)]


def finish_kernel(fold, *refs):
    parts, out = refs[:fold], refs[fold]
    _, _, b = place(fold)
    cols = parts[0].shape[1]
    for e in range(fold):
        value = parts[0][...]
        for d in range(1, fold):
            value = jnp.where((b ^ e) == d, parts[d][...], value)
        out[:, e * cols : (e + 1) * cols] = value


def coeff_kernel(count, fold, *refs):
    coeffs, factors, col_factors = refs[:3]
    blocks, mirrored = refs[3 : 3 + count], refs[3 + count : 4 + count + fold]
    chunks, (out, high, low) = refs[4 + count + fold : -3], refs[-3:]
    r, q, b = place(fold)
    assemble(chunks, high, low, fold, q, b)
    features = blocks[0][...]
    for t in range(1, count):
        features = jnp.where((r ^ q) == t, blocks[t][...], features)
    features = split(features)
    right = split(col_factors[...])
    rows = mirrored[0].shape[0]
    for e in range(fold):
        at = slice(e * rows, (e + 1) * rows)
        crossed = ((r ^ q) & (count // 2)) != 0
        turned = jnp.where(crossed, mirrored[1][...], mirrored[0][...])
        for d in range(1, fold):
            turned = jnp.where((b ^ e) == d, mirrored[d + 1][...], turned)
        turned = turned.T
        own = coeffs[at]
        symmetric = 0.5 * (own * own + turned * turned)
        relation = symmetric - dot3(split(factors[at]), right, 1, 1)
        outer = dot3((high[at], low[at]), features, 1, 1)
        out[at] = outer + 2.0 * own * relation


def per_device(coeffs, features, factors):
    row_count = lax.axis_size("row")
    col_count = lax.axis_size("col")
    fold = col_count // row_count
    own_rows, own_cols = coeffs.shape
    width = features.shape[1]
    quarter = own_rows // row_count
    piece = quarter // fold
    bits = [1 << n for n in range(row_count.bit_length() - 1)]
    every, both = range(row_count), range(fold)

    def send(value, route):
        pairs = []
        for i in every:
            for j in every:
                for k in both:
                    to = route(i, j, k)
                    if to is not None:
                        start = i * col_count + j * fold + k
                        pairs.append((start, to[0] * col_count + to[1] * fold + to[2]))
        return lax.ppermute(value, AXES, pairs)

    b = lax.axis_index("col") % fold
    blocks = {0: lax.dynamic_slice_in_dim(features, b * own_cols, own_cols, 0)}
    for bit in reversed(bits):
        for t in list(blocks):
            blocks[t | bit] = send(blocks[t], lambda i, j, k: (i ^ bit, j, k))
    blocks = [blocks[t] for t in every]

    cuts = [(0, quarter, lambda r, q, b, s=s: q ^ s) for s in every]
    cuts += [(0, own_cols, lambda r, q, b, d=d: b ^ d) for d in both]
    cuts += [(1, own_cols, lambda r, q, b: b)]
    cut = cut_rows([coeffs, factors], cuts, fold)
    parts, turns, col_factors = cut[:row_count], cut[row_count:-1], cut[-1]
    parts = [send(parts[s], lambda i, j, k: (i, j ^ s, k)) if s else parts[s] for s in every]

    turns = [send(turns[d], lambda i, j, k: (i, j, k ^ d)) if d else turns[d] for d in both]

    far = row_count // 2
    hopped = send(turns[0], lambda i, j, k: (i ^ far, j, k) if (i ^ j) & far else None)
    mirrored = [
        send(turns[0], lambda i, j, k: None if (i ^ j) & far else (j, i, k)),
        send(hopped, lambda i, j, k: None if (i ^ j) & far else (j, i ^ far, k)),
        *(send(turns[d], lambda i, j, k: (j, i, k)) for d in both if d),
    ]

    shares = call(
        functools.partial(residual_kernel, row_count, fold),
        [shape(piece, width)] * fold,
        [*parts, *blocks],
        scratch=[pltpu.VMEM((quarter, width), F32)],
        flops=6 * quarter * row_count * own_cols * width,
        grant=12,
    )
    share = shares[0]
    for d in range(1, fold):
        got = send(shares[d], lambda i, j, k: (i, j, k ^ d))
        share = call(add_kernel, [shape(piece, width)], [share, got])[0]

    for bit in reversed(bits):
        got = send(
            col_factors, lambda i, j, k: (i ^ bit, j, k) if (i ^ j) & (2 * bit - 1) == 0 else None
        )
        picked = functools.partial(pick_kernel, bit, fold)
        col_factors = call(picked, [shape(*got.shape)], [col_factors, got])[0]

    chunks = {0: share}
    for bit in reversed(bits):
        for s in list(chunks):
            chunks[s | bit] = send(chunks[s], lambda i, j, k: (i, j ^ bit, k))
    chunks = [chunks[s] for s in every]
    spread = []
    for s in every:
        for d in both:
            one = chunks[s]
            spread.append(send(one, lambda i, j, k: (i, j, k ^ d)) if d else one)

    halves = [pltpu.VMEM((own_rows, width), BF16)] * 2
    give, keep = call(
        functools.partial(project_kernel, row_count, fold),
        [shape(width // 2, own_cols)] * 2,
        [*spread, coeffs],
        scratch=[pltpu.VMEM((width, own_cols), F32), *halves],
        flops=6 * own_rows * own_cols * width,
        grant=12,
    )
    for bit in bits:
        got = send(give, lambda i, j, k: (i ^ bit, j, k))
        rows = got.shape[0]
        total = pltpu.VMEM((rows, own_cols), F32)
        if bit != bits[-1]:
            give, keep = call(
                functools.partial(halve_kernel, 2 * bit, fold),
                [shape(rows // 2, own_cols)] * 2,
                [keep, got],
                scratch=[total],
            )
    pieces = call(
        functools.partial(share_kernel, fold),
        [shape(rows // fold, own_cols)] * fold,
        [keep, got],
        scratch=[total],
    )

    def turned(i):
        out = 0
        for bit in bits:
            out = 2 * out + (i // bit) % 2
        return out

    placed = [send(pieces[d], lambda i, j, k: (j, turned(i), k ^ d)) for d in both]
    grad_features = call(
        functools.partial(finish_kernel, fold), [shape(rows // fold, own_rows)], placed
    )[0].T

    grad_coeffs = call(
        functools.partial(coeff_kernel, row_count, fold),
        [shape(own_rows, own_cols)],
        [coeffs, factors, col_factors, *blocks, *mirrored, *spread],
        scratch=halves,
        flops=6 * own_rows * own_cols * (width + factors.shape[1]),
        grant=12,
    )[0]
    return (grad_coeffs, grad_features)


def solution(mesh):
    in_specs = (P("row", "col"), P("row", None), P("row", None))
    out_specs = (P("row", "col"), P("row", "col"))
    return jax.shard_map(
        per_device, mesh=mesh, in_specs=in_specs, out_specs=out_specs, check_vma=False
    )
```

```python
import functools
import jax
import jax.numpy as jnp
from jax import lax
from jax.experimental import pallas as pl
from jax.experimental.pallas import tpu as pltpu
from jax.sharding import PartitionSpec as P


AXES = ("row", "col")
F32, BF16 = jnp.float32, jnp.bfloat16


def split(value):
    high = value.astype(BF16)
    return high, (value - high.astype(F32)).astype(BF16)


def dot3(left, right, left_dim, right_dim):
    def one(a, b):
        return lax.dot_general(
            a, b, (((left_dim,), (right_dim,)), ((), ())), preferred_element_type=F32
        )

    return one(left[0], right[0]) + (one(left[0], right[1]) + one(left[1], right[0]))


def place(fold):
    col = lax.axis_index("col")
    return lax.axis_index("row"), lax.div(col, fold), lax.rem(col, fold)


def identity(first, shape):
    rows = lax.broadcasted_iota(jnp.int32, shape, 0)
    cols = lax.broadcasted_iota(jnp.int32, shape, 1)
    return jnp.where(rows - cols == first, 1.0, 0.0)


def rows_at(start, count):
    return pl.ds(pl.multiple_of(start, count), count)


def call(kernel, outs, args, scratch=(), flops=0, hbm=(), grant=2):
    moved = sum(4 * a.size for a in args) + sum(4 * o.size for o in outs)
    spaces = [pltpu.HBM if n in hbm else pltpu.VMEM for n in range(len(args))]
    return pl.pallas_call(
        kernel,
        out_shape=outs,
        in_specs=[pl.BlockSpec(memory_space=space) for space in spaces],
        out_specs=[pl.BlockSpec(memory_space=pltpu.VMEM) for _ in outs],
        scratch_shapes=list(scratch),
        compiler_params=pltpu.CompilerParams(vmem_limit_bytes=grant << 20),
        cost_estimate=pl.CostEstimate(flops=flops, bytes_accessed=moved, transcendentals=0),
    )(*args)


def shape(*dims, dtype=F32):
    return jax.ShapeDtypeStruct(dims, dtype)


def cut_kernel(cuts, fold, *refs):
    count = max(cut[0] for cut in cuts) + 1
    ins, outs, sems = refs[:count], refs[count:-1], refs[-1]
    r, q, b = place(fold)
    copies = []
    for n, (source, rows, block) in enumerate(cuts):
        copies.append(
            pltpu.make_async_copy(
                ins[source].at[rows_at(block(r, q, b) * rows, rows)], outs[n], sems.at[n]
            )
        )
    for copy in copies:
        copy.start()
    for copy in copies:
        copy.wait()


def cut_rows(arrays, cuts, fold):
    outs = [shape(rows, arrays[source].shape[1]) for source, rows, _ in cuts]
    return call(
        functools.partial(cut_kernel, cuts, fold),
        outs,
        arrays,
        scratch=[pltpu.SemaphoreType.DMA((len(cuts),))],
        hbm=range(len(arrays)),
    )


def residual_kernel(count, fold, *refs):
    parts, blocks, outs, total = refs[:count], refs[count : 2 * count], refs[2 * count : -1], refs[-1]
    r, q, b = place(fold)
    quarter, own_cols = parts[0].shape
    piece = quarter // fold
    for t in range(count):
        wanted = q ^ r ^ t
        left = parts[0][...]
        for s in range(1, count):
            left = jnp.where(wanted == s, parts[s][...], left)
        if t == 0:
            left = left - identity(b * own_cols - q * quarter, left.shape)
        product = dot3(split(left), split(blocks[t][...]), 1, 0)
        if t == 0:
            total[...] = product
        else:
            total[...] += product
    for d in range(fold):
        outs[d][...] = total[rows_at((b ^ d) * piece, piece)]


def assemble(chunks, high, low, fold, q, b):
    piece = chunks[0].shape[0]
    for n, chunk in enumerate(chunks):
        at = rows_at(((q ^ (n // fold)) * fold + (b ^ (n % fold))) * piece, piece)
        high[at], low[at] = split(chunk[...])


def add_kernel(left, right, out):
    out[...] = left[...] + right[...]


def pick_kernel(bit, fold, old_ref, got_ref, out):
    r, q, _ = place(fold)
    out[...] = jnp.where(((r ^ q) & (2 * bit - 1)) == bit, got_ref[...], old_ref[...])


def project_kernel(count, fold, *refs):
    chunks, coeffs = refs[: count * fold], refs[count * fold]
    give, keep, total, high, low = refs[count * fold + 1 :]
    r, q, b = place(fold)
    assemble(chunks, high, low, fold, q, b)
    own_rows, own_cols = coeffs.shape
    less_one = coeffs[...] - identity((q * fold + b) * own_cols - r * own_rows, coeffs.shape)
    total[...] = dot3((high[...], low[...]), split(less_one), 0, 0)
    half = give.shape[0]
    mine = r & 1
    give[...] = total[rows_at((1 - mine) * half, half)]
    keep[...] = total[rows_at(mine * half, half)]


def halve_kernel(bit, fold, flip, old_ref, got_ref, *refs):
    outs, total = refs[:-1], refs[-1]
    r, _, b = place(fold)
    total[...] = old_ref[...] + got_ref[...]
    pieces = len(outs) // 2
    rows = outs[0].shape[0]
    mine = lax.rem(lax.div(r, bit), 2)
    if flip:
        mine = 1 - mine
    for n, side in enumerate((1 - mine, mine)):
        for d in range(pieces):
            part = b ^ d if pieces > 1 else 0
            outs[n * pieces + d][...] = total[rows_at((side * pieces + part) * rows, rows)]


def join_kernel(fold, *refs):
    parts, out = refs[:-1], refs[-1]
    _, _, b = place(fold)
    cols = parts[0].shape[1]
    sums = [parts[2 * d][...] + parts[2 * d + 1][...] for d in range(fold)]
    for e in range(fold):
        value = sums[0]
        for d in range(1, fold):
            value = jnp.where((b ^ e) == d, sums[d], value)
        out[:, e * cols : (e + 1) * cols] = value


def coeff_kernel(count, fold, *refs):
    coeffs, factors, col_factors = refs[:3]
    blocks, mirrored = refs[3 : 3 + count], refs[3 + count : 3 + count + fold]
    chunks, (out, high, low) = refs[3 + count + fold : -3], refs[-3:]
    r, q, b = place(fold)
    assemble(chunks, high, low, fold, q, b)
    features = blocks[0][...]
    for t in range(1, count):
        features = jnp.where((r ^ q) == t, blocks[t][...], features)
    features = split(features)
    right = split(col_factors[...])
    rows = mirrored[0].shape[0]
    for e in range(fold):
        at = slice(e * rows, (e + 1) * rows)
        turned = mirrored[0][...]
        for d in range(1, fold):
            turned = jnp.where((b ^ e) == d, mirrored[d][...], turned)
        turned = turned.T
        own = coeffs[at]
        symmetric = 0.5 * (own * own + turned * turned)
        relation = symmetric - dot3(split(factors[at]), right, 1, 1)
        outer = dot3((high[at], low[at]), features, 1, 1)
        out[at] = outer + 2.0 * own * relation


def per_device(coeffs, features, factors):
    row_count = lax.axis_size("row")
    col_count = lax.axis_size("col")
    fold = col_count // row_count
    own_rows, own_cols = coeffs.shape
    width = features.shape[1]
    quarter = own_rows // row_count
    piece = quarter // fold
    bits = [1 << n for n in range(row_count.bit_length() - 1)]
    every, both = range(row_count), range(fold)

    def send(value, route):
        pairs = []
        for i in every:
            for j in every:
                for k in both:
                    to = route(i, j, k)
                    if to is not None:
                        start = i * col_count + j * fold + k
                        pairs.append((start, to[0] * col_count + to[1] * fold + to[2]))
        return lax.ppermute(value, AXES, pairs)

    b = lax.axis_index("col") % fold
    blocks = {0: lax.dynamic_slice_in_dim(features, b * own_cols, own_cols, 0)}
    for bit in reversed(bits):
        for t in list(blocks):
            blocks[t | bit] = send(blocks[t], lambda i, j, k: (i ^ bit, j, k))
    blocks = [blocks[t] for t in every]

    cuts = [(0, quarter, lambda r, q, b, s=s: q ^ s) for s in every]
    cuts += [(0, own_cols, lambda r, q, b, d=d: b ^ d) for d in both]
    cuts += [(1, own_cols, lambda r, q, b: b)]
    cut = cut_rows([coeffs, factors], cuts, fold)
    parts, turns, col_factors = cut[:row_count], cut[row_count:-1], cut[-1]
    parts = [send(parts[s], lambda i, j, k: (i, j ^ s, k)) if s else parts[s] for s in every]

    turns = [send(turns[d], lambda i, j, k: (i, j, k ^ d)) if d else turns[d] for d in both]

    mirrored = [send(turns[d], lambda i, j, k: (j, i, k)) for d in both]

    shares = call(
        functools.partial(residual_kernel, row_count, fold),
        [shape(piece, width)] * fold,
        [*parts, *blocks],
        scratch=[pltpu.VMEM((quarter, width), F32)],
        flops=6 * quarter * row_count * own_cols * width,
        grant=12,
    )
    share = shares[0]
    for d in range(1, fold):
        got = send(shares[d], lambda i, j, k: (i, j, k ^ d))
        share = call(add_kernel, [shape(piece, width)], [share, got])[0]

    for bit in reversed(bits):
        got = send(col_factors, lambda i, j, k: (i ^ bit, j, k))
        picked = functools.partial(pick_kernel, bit, fold)
        col_factors = call(picked, [shape(*got.shape)], [col_factors, got])[0]

    chunks = {0: share}
    for bit in reversed(bits):
        for s in list(chunks):
            chunks[s | bit] = send(chunks[s], lambda i, j, k: (i, j ^ bit, k))
    chunks = [chunks[s] for s in every]
    spread = []
    for s in every:
        for d in both:
            one = chunks[s]
            spread.append(send(one, lambda i, j, k: (i, j, k ^ d)) if d else one)

    halves = [pltpu.VMEM((own_rows, width), BF16)] * 2
    give, keep = call(
        functools.partial(project_kernel, row_count, fold),
        [shape(width // 2, own_cols)] * 2,
        [*spread, coeffs],
        scratch=[pltpu.VMEM((width, own_cols), F32), *halves],
        flops=6 * own_rows * own_cols * width,
        grant=12,
    )
    rows = width // 2
    for bit in bits[:-1]:
        got = send(give, lambda i, j, k: (i ^ bit, j, k))
        last = 2 * bit == bits[-1]
        count = fold if last else 1
        halved = call(
            functools.partial(halve_kernel, 2 * bit, fold, last),
            [shape(rows // (2 * count), own_cols)] * (2 * count),
            [keep, got],
            scratch=[pltpu.VMEM((rows, own_cols), F32)],
        )
        rows //= 2
        give, keep = halved[0], halved[1]
    gives, keeps = halved[:fold], halved[fold:]
    parts = []
    for d in both:
        far = bits[-1]
        parts += [
            send(keeps[d], lambda i, j, k: (i, j, k ^ d)) if d else keeps[d],
            send(gives[d], lambda i, j, k: (i ^ far, j, k ^ d)),
        ]
    joined = call(functools.partial(join_kernel, fold), [shape(rows // fold, own_rows)], parts)[0]

    def portion(i):
        out = 0
        for bit in bits:
            out = 2 * out + (i // bit) % 2
        return out ^ 1

    grad_features = send(joined, lambda i, j, k: (j, portion(i), k)).T

    grad_coeffs = call(
        functools.partial(coeff_kernel, row_count, fold),
        [shape(own_rows, own_cols)],
        [coeffs, factors, col_factors, *blocks, *mirrored, *spread],
        scratch=halves,
        flops=6 * own_rows * own_cols * (width + factors.shape[1]),
        grant=12,
    )[0]
    return (grad_coeffs, grad_features)


def solution(mesh):
    in_specs = (P("row", "col"), P("row", None), P("row", None))
    out_specs = (P("row", "col"), P("row", "col"))
    return jax.shard_map(
        per_device, mesh=mesh, in_specs=in_specs, out_specs=out_specs, check_vma=False
    )
```

```python
import functools
import jax
import jax.numpy as jnp
from jax import lax
from jax.experimental import pallas as pl
from jax.experimental.pallas import tpu as pltpu
from jax.sharding import PartitionSpec as P


AXES = ("row", "col")
F32, BF16 = jnp.float32, jnp.bfloat16


def split(value):
    high = value.astype(BF16)
    return high, (value - high.astype(F32)).astype(BF16)


def dot3(left, right, left_dim, right_dim):
    def one(a, b):
        return lax.dot_general(
            a, b, (((left_dim,), (right_dim,)), ((), ())), preferred_element_type=F32
        )

    return one(left[0], right[0]) + (one(left[0], right[1]) + one(left[1], right[0]))


def place(fold):
    col = lax.axis_index("col")
    return lax.axis_index("row"), lax.div(col, fold), lax.rem(col, fold)


def identity(first, shape):
    rows = lax.broadcasted_iota(jnp.int32, shape, 0)
    cols = lax.broadcasted_iota(jnp.int32, shape, 1)
    return jnp.where(rows - cols == first, 1.0, 0.0)


def rows_at(start, count):
    return pl.ds(pl.multiple_of(start, count), count)


def call(kernel, outs, args, scratch=(), flops=0, hbm=(), grant=2):
    moved = sum(4 * a.size for a in args) + sum(4 * o.size for o in outs)
    spaces = [pltpu.HBM if n in hbm else pltpu.VMEM for n in range(len(args))]
    return pl.pallas_call(
        kernel,
        out_shape=outs,
        in_specs=[pl.BlockSpec(memory_space=space) for space in spaces],
        out_specs=[pl.BlockSpec(memory_space=pltpu.VMEM) for _ in outs],
        scratch_shapes=list(scratch),
        compiler_params=pltpu.CompilerParams(vmem_limit_bytes=grant << 20),
        cost_estimate=pl.CostEstimate(flops=flops, bytes_accessed=moved, transcendentals=0),
    )(*args)


def shape(*dims, dtype=F32):
    return jax.ShapeDtypeStruct(dims, dtype)


def cut_kernel(cuts, fold, *refs):
    count = max(cut[0] for cut in cuts) + 1
    ins, outs, sems = refs[:count], refs[count:-1], refs[-1]
    r, q, b = place(fold)
    copies = []
    for n, (source, rows, block) in enumerate(cuts):
        copies.append(
            pltpu.make_async_copy(
                ins[source].at[rows_at(block(r, q, b) * rows, rows)], outs[n], sems.at[n]
            )
        )
    for copy in copies:
        copy.start()
    for copy in copies:
        copy.wait()


def cut_rows(arrays, cuts, fold):
    outs = [shape(rows, arrays[source].shape[1]) for source, rows, _ in cuts]
    return call(
        functools.partial(cut_kernel, cuts, fold),
        outs,
        arrays,
        scratch=[pltpu.SemaphoreType.DMA((len(cuts),))],
        hbm=range(len(arrays)),
    )


def residual_kernel(count, fold, *refs):
    parts, blocks, outs, total = refs[:count], refs[count : 2 * count], refs[2 * count : -1], refs[-1]
    r, q, b = place(fold)
    quarter, own_cols = parts[0].shape
    piece = quarter // fold
    for t in range(count):
        wanted = q ^ r ^ t
        left = parts[0][...]
        for s in range(1, count):
            left = jnp.where(wanted == s, parts[s][...], left)
        if t == 0:
            left = left - identity(b * own_cols - q * quarter, left.shape)
        product = dot3(split(left), split(blocks[t][...]), 1, 0)
        if t == 0:
            total[...] = product
        else:
            total[...] += product
    for d in range(fold):
        outs[d][...] = total[rows_at((b ^ d) * piece, piece)]


def assemble(chunks, high, low, fold, q, b):
    piece = chunks[0].shape[0]
    for n, chunk in enumerate(chunks):
        at = rows_at(((q ^ (n // fold)) * fold + (b ^ (n % fold))) * piece, piece)
        high[at], low[at] = split(chunk[...])


def add_kernel(left, right, out):
    out[...] = left[...] + right[...]


def pick_kernel(bit, fold, old_ref, got_ref, out):
    r, q, _ = place(fold)
    out[...] = jnp.where(((r ^ q) & (2 * bit - 1)) == bit, got_ref[...], old_ref[...])


def project_kernel(count, fold, *refs):
    chunks, coeffs = refs[: count * fold], refs[count * fold]
    give, keep, total, high, low = refs[count * fold + 1 :]
    r, q, b = place(fold)
    assemble(chunks, high, low, fold, q, b)
    own_rows, own_cols = coeffs.shape
    less_one = coeffs[...] - identity((q * fold + b) * own_cols - r * own_rows, coeffs.shape)
    total[...] = dot3((high[...], low[...]), split(less_one), 0, 0)
    half = give.shape[0]
    mine = r & 1
    give[...] = total[rows_at((1 - mine) * half, half)]
    keep[...] = total[rows_at(mine * half, half)]


def halve_kernel(bit, fold, flip, old_ref, got_ref, *refs):
    outs, total = refs[:-1], refs[-1]
    r, _, b = place(fold)
    total[...] = old_ref[...] + got_ref[...]
    pieces = len(outs) // 2
    rows = outs[0].shape[0]
    mine = lax.rem(lax.div(r, bit), 2)
    if flip:
        mine = 1 - mine
    for n, side in enumerate((1 - mine, mine)):
        for d in range(pieces):
            part = b ^ d if pieces > 1 else 0
            outs[n * pieces + d][...] = total[rows_at((side * pieces + part) * rows, rows)]


def join_kernel(fold, *refs):
    parts, out = refs[:-1], refs[-1]
    _, _, b = place(fold)
    cols = parts[0].shape[1]
    sums = [parts[2 * d][...] + parts[2 * d + 1][...] for d in range(fold)]
    for e in range(fold):
        value = sums[0]
        for d in range(1, fold):
            value = jnp.where((b ^ e) == d, sums[d], value)
        out[:, e * cols : (e + 1) * cols] = value


def coeff_kernel(count, fold, *refs):
    coeffs, factors, col_factors = refs[:3]
    blocks, mirrored = refs[3 : 3 + count], refs[3 + count : 4 + count + fold]
    chunks, (out, high, low) = refs[4 + count + fold : -3], refs[-3:]
    r, q, b = place(fold)
    assemble(chunks, high, low, fold, q, b)
    features = blocks[0][...]
    for t in range(1, count):
        features = jnp.where((r ^ q) == t, blocks[t][...], features)
    features = split(features)
    right = split(col_factors[...])
    rows = mirrored[0].shape[0]
    for e in range(fold):
        at = slice(e * rows, (e + 1) * rows)
        crossed = ((r ^ q) & (count // 2)) != 0
        turned = jnp.where(crossed, mirrored[1][...], mirrored[0][...])
        for d in range(1, fold):
            turned = jnp.where((b ^ e) == d, mirrored[d + 1][...], turned)
        turned = turned.T
        own = coeffs[at]
        symmetric = 0.5 * (own * own + turned * turned)
        relation = symmetric - dot3(split(factors[at]), right, 1, 1)
        outer = dot3((high[at], low[at]), features, 1, 1)
        out[at] = outer + 2.0 * own * relation


def per_device(coeffs, features, factors):
    row_count = lax.axis_size("row")
    col_count = lax.axis_size("col")
    fold = col_count // row_count
    own_rows, own_cols = coeffs.shape
    width = features.shape[1]
    quarter = own_rows // row_count
    piece = quarter // fold
    bits = [1 << n for n in range(row_count.bit_length() - 1)]
    every, both = range(row_count), range(fold)

    def send(value, route):
        pairs = []
        for i in every:
            for j in every:
                for k in both:
                    to = route(i, j, k)
                    if to is not None:
                        start = i * col_count + j * fold + k
                        pairs.append((start, to[0] * col_count + to[1] * fold + to[2]))
        return lax.ppermute(value, AXES, pairs)

    b = lax.axis_index("col") % fold
    blocks = {0: lax.dynamic_slice_in_dim(features, b * own_cols, own_cols, 0)}
    for bit in reversed(bits):
        for t in list(blocks):
            blocks[t | bit] = send(blocks[t], lambda i, j, k: (i ^ bit, j, k))
    blocks = [blocks[t] for t in every]

    cuts = [(0, quarter, lambda r, q, b, s=s: q ^ s) for s in every]
    cuts += [(0, own_cols, lambda r, q, b, d=d: b ^ d) for d in both]
    cuts += [(1, own_cols, lambda r, q, b: b)]
    cut = cut_rows([coeffs, factors], cuts, fold)
    parts, turns, col_factors = cut[:row_count], cut[row_count:-1], cut[-1]
    parts = [send(parts[s], lambda i, j, k: (i, j ^ s, k)) if s else parts[s] for s in every]

    turns = [send(turns[d], lambda i, j, k: (i, j, k ^ d)) if d else turns[d] for d in both]

    far = row_count // 2
    hopped = send(turns[0], lambda i, j, k: (i ^ far, j, k))
    mirrored = [
        send(turns[0], lambda i, j, k: (i, j, k) if (i ^ j) & far else (j, i, k)),
        send(hopped, lambda i, j, k: None if (i ^ j) & far else (j, i ^ far, k)),
        *(send(turns[d], lambda i, j, k: (j, i, k)) for d in both if d),
    ]

    shares = call(
        functools.partial(residual_kernel, row_count, fold),
        [shape(piece, width)] * fold,
        [*parts, *blocks],
        scratch=[pltpu.VMEM((quarter, width), F32)],
        flops=6 * quarter * row_count * own_cols * width,
        grant=12,
    )
    share = shares[0]
    for d in range(1, fold):
        got = send(shares[d], lambda i, j, k: (i, j, k ^ d))
        share = call(add_kernel, [shape(piece, width)], [share, got])[0]

    for bit in reversed(bits):
        got = send(col_factors, lambda i, j, k: (i ^ bit, j, k))
        picked = functools.partial(pick_kernel, bit, fold)
        col_factors = call(picked, [shape(*got.shape)], [col_factors, got])[0]

    chunks = {0: share}
    for bit in reversed(bits):
        for s in list(chunks):
            chunks[s | bit] = send(chunks[s], lambda i, j, k: (i, j ^ bit, k))
    chunks = [chunks[s] for s in every]
    spread = []
    for s in every:
        for d in both:
            one = chunks[s]
            spread.append(send(one, lambda i, j, k: (i, j, k ^ d)) if d else one)

    halves = [pltpu.VMEM((own_rows, width), BF16)] * 2
    give, keep = call(
        functools.partial(project_kernel, row_count, fold),
        [shape(width // 2, own_cols)] * 2,
        [*spread, coeffs],
        scratch=[pltpu.VMEM((width, own_cols), F32), *halves],
        flops=6 * own_rows * own_cols * width,
        grant=12,
    )
    rows = width // 2
    for bit in bits[:-1]:
        got = send(give, lambda i, j, k: (i ^ bit, j, k))
        last = 2 * bit == bits[-1]
        count = fold if last else 1
        halved = call(
            functools.partial(halve_kernel, 2 * bit, fold, last),
            [shape(rows // (2 * count), own_cols)] * (2 * count),
            [keep, got],
            scratch=[pltpu.VMEM((rows, own_cols), F32)],
        )
        rows //= 2
        give, keep = halved[0], halved[1]
    gives, keeps = halved[:fold], halved[fold:]
    parts = []
    for d in both:
        far = bits[-1]
        parts += [
            send(keeps[d], lambda i, j, k: (i, j, k ^ d)) if d else keeps[d],
            send(gives[d], lambda i, j, k: (i ^ far, j, k ^ d)),
        ]
    joined = call(functools.partial(join_kernel, fold), [shape(rows // fold, own_rows)], parts)[0]

    def portion(i):
        out = 0
        for bit in bits:
            out = 2 * out + (i // bit) % 2
        return out ^ 1

    grad_features = send(joined, lambda i, j, k: (j, portion(i), k)).T

    grad_coeffs = call(
        functools.partial(coeff_kernel, row_count, fold),
        [shape(own_rows, own_cols)],
        [coeffs, factors, col_factors, *blocks, *mirrored, *spread],
        scratch=halves,
        flops=6 * own_rows * own_cols * (width + factors.shape[1]),
        grant=12,
    )[0]
    return (grad_coeffs, grad_features)


def solution(mesh):
    in_specs = (P("row", "col"), P("row", None), P("row", None))
    out_specs = (P("row", "col"), P("row", "col"))
    return jax.shard_map(
        per_device, mesh=mesh, in_specs=in_specs, out_specs=out_specs, check_vma=False
    )
```

```python
import functools
import jax
import jax.numpy as jnp
from jax import lax
from jax.experimental import pallas as pl
from jax.experimental.pallas import tpu as pltpu
from jax.sharding import PartitionSpec as P


AXES = ("row", "col")
F32, BF16 = jnp.float32, jnp.bfloat16


def split(value):
    high = value.astype(BF16)
    return high, (value - high.astype(F32)).astype(BF16)


def dot3(left, right, left_dim, right_dim):
    def one(a, b):
        return lax.dot_general(
            a, b, (((left_dim,), (right_dim,)), ((), ())), preferred_element_type=F32
        )

    return one(left[0], right[0]) + (one(left[0], right[1]) + one(left[1], right[0]))


def place(fold):
    col = lax.axis_index("col")
    return lax.axis_index("row"), lax.div(col, fold), lax.rem(col, fold)


def identity(first, shape):
    rows = lax.broadcasted_iota(jnp.int32, shape, 0)
    cols = lax.broadcasted_iota(jnp.int32, shape, 1)
    return jnp.where(rows - cols == first, 1.0, 0.0)


def rows_at(start, count):
    return pl.ds(pl.multiple_of(start, count), count)


def call(kernel, outs, args, scratch=(), flops=0, hbm=(), grant=2):
    moved = sum(4 * a.size for a in args) + sum(4 * o.size for o in outs)
    spaces = [pltpu.HBM if n in hbm else pltpu.VMEM for n in range(len(args))]
    return pl.pallas_call(
        kernel,
        out_shape=outs,
        in_specs=[pl.BlockSpec(memory_space=space) for space in spaces],
        out_specs=[pl.BlockSpec(memory_space=pltpu.VMEM) for _ in outs],
        scratch_shapes=list(scratch),
        compiler_params=pltpu.CompilerParams(vmem_limit_bytes=grant << 20),
        cost_estimate=pl.CostEstimate(flops=flops, bytes_accessed=moved, transcendentals=0),
    )(*args)


def shape(*dims, dtype=F32):
    return jax.ShapeDtypeStruct(dims, dtype)


def cut_kernel(cuts, fold, *refs):
    count = max(cut[0] for cut in cuts) + 1
    ins, outs, sems = refs[:count], refs[count:-1], refs[-1]
    r, q, b = place(fold)
    copies = []
    for n, (source, rows, block) in enumerate(cuts):
        copies.append(
            pltpu.make_async_copy(
                ins[source].at[rows_at(block(r, q, b) * rows, rows)], outs[n], sems.at[n]
            )
        )
    for copy in copies:
        copy.start()
    for copy in copies:
        copy.wait()


def cut_rows(arrays, cuts, fold):
    outs = [shape(rows, arrays[source].shape[1]) for source, rows, _ in cuts]
    return call(
        functools.partial(cut_kernel, cuts, fold),
        outs,
        arrays,
        scratch=[pltpu.SemaphoreType.DMA((len(cuts),))],
        hbm=range(len(arrays)),
    )


def residual_kernel(count, fold, *refs):
    parts, blocks, outs, total = refs[:count], refs[count : 2 * count], refs[2 * count : -1], refs[-1]
    r, q, b = place(fold)
    quarter, own_cols = parts[0].shape
    piece = quarter // fold
    for t in range(count):
        wanted = q ^ r ^ t
        left = parts[0][...]
        for s in range(1, count):
            left = jnp.where(wanted == s, parts[s][...], left)
        if t == 0:
            left = left - identity(b * own_cols - q * quarter, left.shape)
        product = dot3(split(left), split(blocks[t][...]), 1, 0)
        if t == 0:
            total[...] = product
        else:
            total[...] += product
    for d in range(fold):
        outs[d][...] = total[rows_at((b ^ d) * piece, piece)]


def assemble(chunks, high, low, fold, q, b):
    piece = chunks[0].shape[0]
    for n, chunk in enumerate(chunks):
        at = rows_at(((q ^ (n // fold)) * fold + (b ^ (n % fold))) * piece, piece)
        high[at], low[at] = split(chunk[...])


def add_kernel(left, right, out):
    out[...] = left[...] + right[...]


def pick_kernel(bit, fold, old_ref, got_ref, out):
    r, q, _ = place(fold)
    out[...] = jnp.where(((r ^ q) & (2 * bit - 1)) == bit, got_ref[...], old_ref[...])


def project_kernel(count, fold, *refs):
    chunks, coeffs = refs[: count * fold - 1], refs[count * fold - 1]
    total, high, low = refs[count * fold :]
    r, q, b = place(fold)
    high[...] = jnp.zeros_like(high)
    low[...] = jnp.zeros_like(low)
    assemble(chunks, high, low, fold, q, b)
    own_rows, own_cols = coeffs.shape
    less_one = coeffs[...] - identity((q * fold + b) * own_cols - r * own_rows, coeffs.shape)
    total[...] = dot3((high[...], low[...]), split(less_one), 0, 0)


def last_kernel(count, fold, chunk, coeffs, part, give, keep, total):
    r, q, b = place(fold)
    own_rows, own_cols = coeffs.shape
    piece = chunk.shape[0]
    start = ((q ^ (count - 1)) * fold + (b ^ (fold - 1))) * piece
    rows = coeffs[rows_at(start, piece)]
    less_one = rows - identity((q * fold + b) * own_cols - r * own_rows - start, rows.shape)
    total[...] = part[...] + dot3(split(chunk[...]), split(less_one), 0, 0)
    half = give.shape[0]
    mine = r & 1
    give[...] = total[rows_at((1 - mine) * half, half)]
    keep[...] = total[rows_at(mine * half, half)]


def halve_kernel(bit, fold, flip, old_ref, got_ref, *refs):
    outs, total = refs[:-1], refs[-1]
    r, _, b = place(fold)
    total[...] = old_ref[...] + got_ref[...]
    pieces = len(outs) // 2
    rows = outs[0].shape[0]
    mine = lax.rem(lax.div(r, bit), 2)
    if flip:
        mine = 1 - mine
    for n, side in enumerate((1 - mine, mine)):
        for d in range(pieces):
            part = b ^ d if pieces > 1 else 0
            outs[n * pieces + d][...] = total[rows_at((side * pieces + part) * rows, rows)]


def join_kernel(fold, *refs):
    parts, out = refs[:-1], refs[-1]
    _, _, b = place(fold)
    cols = parts[0].shape[1]
    sums = [parts[2 * d][...] + parts[2 * d + 1][...] for d in range(fold)]
    for e in range(fold):
        value = sums[0]
        for d in range(1, fold):
            value = jnp.where((b ^ e) == d, sums[d], value)
        out[:, e * cols : (e + 1) * cols] = value


def coeff_kernel(count, fold, *refs):
    coeffs, factors, col_factors = refs[:3]
    blocks, mirrored = refs[3 : 3 + count], refs[3 + count : 4 + count + fold]
    chunks, (out, high, low) = refs[4 + count + fold : -3], refs[-3:]
    r, q, b = place(fold)
    assemble(chunks, high, low, fold, q, b)
    features = blocks[0][...]
    for t in range(1, count):
        features = jnp.where((r ^ q) == t, blocks[t][...], features)
    features = split(features)
    right = split(col_factors[...])
    rows = mirrored[0].shape[0]
    for e in range(fold):
        at = slice(e * rows, (e + 1) * rows)
        crossed = ((r ^ q) & (count // 2)) != 0
        turned = jnp.where(crossed, mirrored[1][...], mirrored[0][...])
        for d in range(1, fold):
            turned = jnp.where((b ^ e) == d, mirrored[d + 1][...], turned)
        turned = turned.T
        own = coeffs[at]
        symmetric = 0.5 * (own * own + turned * turned)
        relation = symmetric - dot3(split(factors[at]), right, 1, 1)
        outer = dot3((high[at], low[at]), features, 1, 1)
        out[at] = outer + 2.0 * own * relation


def per_device(coeffs, features, factors):
    row_count = lax.axis_size("row")
    col_count = lax.axis_size("col")
    fold = col_count // row_count
    own_rows, own_cols = coeffs.shape
    width = features.shape[1]
    quarter = own_rows // row_count
    piece = quarter // fold
    bits = [1 << n for n in range(row_count.bit_length() - 1)]
    every, both = range(row_count), range(fold)

    def send(value, route):
        pairs = []
        for i in every:
            for j in every:
                for k in both:
                    to = route(i, j, k)
                    if to is not None:
                        start = i * col_count + j * fold + k
                        pairs.append((start, to[0] * col_count + to[1] * fold + to[2]))
        return lax.ppermute(value, AXES, pairs)

    b = lax.axis_index("col") % fold
    blocks = {0: lax.dynamic_slice_in_dim(features, b * own_cols, own_cols, 0)}
    for bit in reversed(bits):
        for t in list(blocks):
            blocks[t | bit] = send(blocks[t], lambda i, j, k: (i ^ bit, j, k))
    blocks = [blocks[t] for t in every]

    cuts = [(0, quarter, lambda r, q, b, s=s: q ^ s) for s in every]
    cuts += [(0, own_cols, lambda r, q, b, d=d: b ^ d) for d in both]
    cuts += [(1, own_cols, lambda r, q, b: b)]
    cut = cut_rows([coeffs, factors], cuts, fold)
    parts, turns, col_factors = cut[:row_count], cut[row_count:-1], cut[-1]
    parts = [send(parts[s], lambda i, j, k: (i, j ^ s, k)) if s else parts[s] for s in every]

    turns = [send(turns[d], lambda i, j, k: (i, j, k ^ d)) if d else turns[d] for d in both]

    far = row_count // 2
    hopped = send(turns[0], lambda i, j, k: (i ^ far, j, k))
    mirrored = [
        send(turns[0], lambda i, j, k: (i, j, k) if (i ^ j) & far else (j, i, k)),
        send(hopped, lambda i, j, k: (i ^ far, j, k) if (i ^ j) & far else (j, i ^ far, k)),
        *(send(turns[d], lambda i, j, k: (j, i, k)) for d in both if d),
    ]

    shares = call(
        functools.partial(residual_kernel, row_count, fold),
        [shape(piece, width)] * fold,
        [*parts, *blocks],
        scratch=[pltpu.VMEM((quarter, width), F32)],
        flops=6 * quarter * row_count * own_cols * width,
        grant=12,
    )
    share = shares[0]
    for d in range(1, fold):
        got = send(shares[d], lambda i, j, k: (i, j, k ^ d))
        share = call(add_kernel, [shape(piece, width)], [share, got])[0]

    for bit in reversed(bits):
        got = send(col_factors, lambda i, j, k: (i ^ bit, j, k))
        picked = functools.partial(pick_kernel, bit, fold)
        col_factors = call(picked, [shape(*got.shape)], [col_factors, got])[0]

    chunks = {0: share}
    for bit in reversed(bits):
        for s in list(chunks):
            chunks[s | bit] = send(chunks[s], lambda i, j, k: (i, j ^ bit, k))
    chunks = [chunks[s] for s in every]
    spread = []
    for s in every:
        for d in both:
            one = chunks[s]
            spread.append(send(one, lambda i, j, k: (i, j, k ^ d)) if d else one)

    halves = [pltpu.VMEM((own_rows, width), BF16)] * 2
    part = call(
        functools.partial(project_kernel, row_count, fold),
        [shape(width, own_cols)],
        [*spread[:-1], coeffs],
        scratch=halves,
        flops=6 * own_rows * own_cols * width,
        grant=12,
    )[0]
    give, keep = call(
        functools.partial(last_kernel, row_count, fold),
        [shape(width // 2, own_cols)] * 2,
        [spread[-1], coeffs, part],
        scratch=[pltpu.VMEM((width, own_cols), F32)],
        flops=6 * piece * own_cols * width,
        grant=6,
    )
    rows = width // 2
    for bit in bits[:-1]:
        got = send(give, lambda i, j, k: (i ^ bit, j, k))
        last = 2 * bit == bits[-1]
        count = fold if last else 1
        halved = call(
            functools.partial(halve_kernel, 2 * bit, fold, last),
            [shape(rows // (2 * count), own_cols)] * (2 * count),
            [keep, got],
            scratch=[pltpu.VMEM((rows, own_cols), F32)],
        )
        rows //= 2
        give, keep = halved[0], halved[1]
    gives, keeps = halved[:fold], halved[fold:]
    parts = []
    for d in both:
        far = bits[-1]
        parts += [
            send(keeps[d], lambda i, j, k: (i, j, k ^ d)) if d else keeps[d],
            send(gives[d], lambda i, j, k: (i ^ far, j, k ^ d)),
        ]
    joined = call(functools.partial(join_kernel, fold), [shape(rows // fold, own_rows)], parts)[0]

    def portion(i):
        out = 0
        for bit in bits:
            out = 2 * out + (i // bit) % 2
        return out ^ 1

    grad_features = send(joined, lambda i, j, k: (j, portion(i), k)).T

    grad_coeffs = call(
        functools.partial(coeff_kernel, row_count, fold),
        [shape(own_rows, own_cols)],
        [coeffs, factors, col_factors, *blocks, *mirrored, *spread],
        scratch=halves,
        flops=6 * own_rows * own_cols * (width + factors.shape[1]),
        grant=12,
    )[0]
    return (grad_coeffs, grad_features)


def solution(mesh):
    in_specs = (P("row", "col"), P("row", None), P("row", None))
    out_specs = (P("row", "col"), P("row", "col"))
    return jax.shard_map(
        per_device, mesh=mesh, in_specs=in_specs, out_specs=out_specs, check_vma=False
    )
```
